256 devices in a mesh: blk: 64 (over y, x_hi, z), repl: 4 (over x_lo, core).
Axes of the slice: x: 4 (x_hi: 2, x_lo: 2; x = x_hi * 2 + x_lo), y: 4, z: 8, core: 2. Of those that a mesh axis runs over, the one named last changes fastest.
Arguments:
- feats: bfloat16 [131072, 512], P(('blk', 'repl')), may hold values from -6 to 6
- weight: bfloat16 [512, 512], replicated, may hold values from -0.25 to 0.25
- tile_vals: bfloat16 [1024, 8, 128, 128], P(('blk', 'repl')), may hold values from -0.25 to 0.25
- tile_cols: int32 [1024, 8], P(('blk', 'repl')), may hold values from 0 to 1023, as said below
- tile_count: int32 [1024], P(('blk', 'repl')), may hold values from 2 to 8, as said below
- cotangent: bfloat16 [131072, 512], P(('blk', 'repl')), may hold values from -24 to 24
Outputs:
- output: bfloat16 [131072, 512], P(('blk', 'repl'))
- weight_grad: float32 [512, 512], replicated
- feat_grad: bfloat16 [131072, 512], P(('blk', 'repl'))
The draws below stay inside these ranges and needn't reach their ends.
Inputs may be any that keep to these rules, and one draw needn't show every extreme that they name: `tile_cols`: slot 0 of block row k names k itself. Every named column block lies in a panel (of 2048 nodes, block row k being in panel k * 128 // 2048) at most 2 panels away from its row's panel, counted around a closed cycle of panels. `tile_count`: slots at and after a block row's count are not part of the adjacency.
All inputs are finite; a program needn't handle non-finite values.
Results may differ from the reference program's by a relative error of at most 0.011.
Values may be sent and summed in bfloat16 or wider, within the bound.
A program may use at most 128 MiB of HBM per device.

```python
import math
import jax
import jax.numpy as jnp

F = 512
TILE = 128
SLOTS = 8
REACH = 2
NODES = 131072
PANEL = 2048
BLOCKS = 1024


def draw_tile_cols(key, part):
    panel_blocks = PANEL // TILE
    panel_count = BLOCKS // panel_blocks
    first_key, second_key, third_key = jax.random.split(key, 3)
    block_row = jnp.arange(BLOCKS, dtype=jnp.int32)
    home_panel = block_row // panel_blocks
    offset = jax.random.randint(first_key, (BLOCKS, SLOTS), -REACH, REACH + 1)
    far_side = jnp.where(jax.random.randint(second_key, (BLOCKS,), 0, 2) == 0, -REACH, REACH)
    offset = offset.at[:, 1].set(far_side)
    inside = jax.random.randint(third_key, (BLOCKS, SLOTS), 0, panel_blocks)
    columns = (home_panel[:, None] + offset) % panel_count * panel_blocks + inside
    columns = columns.at[:, 0].set(block_row)
    return columns.astype(jnp.int32)


def draw_tile_count(key, part):
    panel_blocks = PANEL // TILE
    panel_count = BLOCKS // panel_blocks
    first_key, second_key, third_key = jax.random.split(key, 3)
    ceiling = jax.random.randint(first_key, (panel_count,), 3, SLOTS + 1)
    counts = jax.random.randint(second_key, (BLOCKS,), 2, SLOTS + 1)
    block_row = jnp.arange(BLOCKS, dtype=jnp.int32)
    counts = jnp.minimum(counts, ceiling[block_row // panel_blocks])
    fullest = jax.random.randint(third_key, (), 0, BLOCKS)
    counts = counts.at[fullest].set(SLOTS)
    return counts.astype(jnp.int32)


def with_spikes(entries, rng, source, target, blocks, factor):
    owner, partner = [(jnp.arange(entries.shape[position]) // (entries.shape[position] // blocks)).reshape([-1 if axis == position else 1 for axis in range(entries.ndim)]) for position in (source, target)]
    chosen = jax.random.permutation(rng, blocks)[partner]
    strong = (owner == chosen) | (owner == (partner + blocks // 2) % blocks)
    return jnp.where(strong, factor * entries, entries)


def block_scale(rng, dims, cuts, smallest, top_value):
    def one(dim, shards_of):
        heights = jax.random.uniform(jax.random.fold_in(jax.random.fold_in(rng, 6), dim), (shards_of,), jnp.float32, smallest / len(cuts), top_value / len(cuts))
        return jnp.repeat(jnp.exp(heights), dims[dim] // shards_of).reshape((-1,) + (1,) * (len(dims) - dim - 1))

    loudness = one(*cuts[0])
    for cut in cuts[1:]:
        loudness = loudness * one(*cut)
    return loudness


def scatter_about(rng, dims, scale, bound, cuts=(), held_as=jnp.bfloat16):
    values = scale * jax.random.normal(rng, dims, jnp.float32)
    if cuts:
        values = values * block_scale(rng, dims, cuts, -0.22, 0.18)
    return jnp.clip(values, -bound, bound).astype(held_as)


def noise_with(key, extent, spread, reach, cuts, heavy, kind=jnp.bfloat16):
    entries = spread * jax.random.normal(key, extent, jnp.float32)
    if cuts:
        entries = entries * block_scale(key, extent, cuts, -0.22, 0.18)
    return jnp.clip(with_spikes(entries, jax.random.fold_in(key, 3), *heavy), -reach, reach).astype(kind)


def setup_inputs(seed: int = 0) -> dict:
    key_of = jax.random.split(jax.random.key(seed), 7)
    feats = scatter_about(key_of[0], (NODES, F), 1.0, 6.0, ((0, 256),))
    weight = scatter_about(key_of[1], (F, F), F ** -0.5, 0.25)
    tile_vals = scatter_about(key_of[2], (BLOCKS, SLOTS, TILE, TILE), (SLOTS * TILE // 2) ** -0.5, 0.25, ((0, 256),))
    tile_cols = draw_tile_cols(jax.random.fold_in(key_of[6], 71), 0)
    tile_count = draw_tile_count(jax.random.fold_in(key_of[6], 71), 0)
    cotangent = noise_with(key_of[5], (NODES, F), 1.0, 24.0, ((0, 256),), (0, 1, 256, 6.0))
    return {"feats": feats, "weight": weight, "tile_vals": tile_vals, "tile_cols": tile_cols, "tile_count": tile_count, "cotangent": cotangent}


def silu_slope(preact):
    sigma = jax.nn.sigmoid(preact)
    return sigma * (1.0 + preact * (1.0 - sigma))

def reference(feats, weight, tile_vals, tile_cols, tile_count, cotangent):
    feat_blocks = feats.reshape(BLOCKS, TILE, F).astype(jnp.float32)
    live_slots = jnp.arange(SLOTS, dtype=jnp.int32)[None, :] < tile_count[:, None]
    summed = jnp.zeros((BLOCKS, TILE, F), jnp.float32)
    for slot_index in range(SLOTS):
        values = jnp.where(live_slots[:, slot_index, None, None], tile_vals[:, slot_index].astype(jnp.float32), jnp.float32(0.0))
        picked = feat_blocks[tile_cols[:, slot_index]]
        summed = summed + jnp.einsum('nij,njf->nif', values, picked)
    aggregate = summed.reshape(NODES, F).astype(jnp.bfloat16)
    preact = jnp.dot(aggregate, weight, preferred_element_type=jnp.float32)
    output = jax.nn.silu(preact).astype(jnp.bfloat16)
    slope = (cotangent.astype(jnp.float32) * silu_slope(preact)).astype(jnp.bfloat16)
    weight_grad = jnp.dot(aggregate.T, slope, preferred_element_type=jnp.float32) * (1.0 / math.sqrt(NODES))
    backward = jnp.dot(slope, weight.T, preferred_element_type=jnp.float32).astype(jnp.bfloat16)
    back_blocks = backward.reshape(BLOCKS, TILE, F).astype(jnp.float32)
    grad_sum = jnp.zeros((BLOCKS, TILE, F), jnp.float32)
    for slot_index in range(SLOTS):
        values = jnp.where(live_slots[:, slot_index, None, None], tile_vals[:, slot_index].astype(jnp.float32), jnp.float32(0.0))
        contrib = jnp.einsum('nji,njf->nif', values, back_blocks)
        grad_sum = grad_sum.at[tile_cols[:, slot_index]].add(contrib)
    feat_grad = grad_sum.reshape(NODES, F).astype(jnp.bfloat16)
    return (output, weight_grad, feat_grad)
```

```python
import functools
import math

import jax
import jax.numpy as jnp
from jax import lax
from jax.experimental import pallas as pl
from jax.experimental.pallas import tpu as pltpu
from jax.sharding import PartitionSpec as P

TILE = 128
SLOTS = 8
REACH = 2
SPAN = 2 * REACH + 1
GROUP = 4
MESH = pl.DeviceIdType.MESH
BF16 = jnp.bfloat16
F32 = jnp.float32
RUN = 8


def place(nb, run):
    b = lax.axis_index("blk")
    r = lax.axis_index("repl")
    flip = 2 * ((b // run) % 2)
    g = (r + flip) % GROUP
    up = (b + 1) % nb
    down = (b + nb - 1) % nb
    r_up = (g + 2 * ((up // run) % 2)) % GROUP
    r_down = (g + 2 * ((down // run) % 2)) % GROUP
    p1 = r + 1 - 2 * (r % 2)
    p2 = (r + 2) % GROUP
    p3 = (p1 + 2) % GROUP
    return b, r, flip, g, up, down, r_up, r_down, p1, p2, p3


def partners(r):
    p1 = r + 1 - 2 * (r % 2)
    return r, p1, (r + 2) % GROUP, (p1 + 2) % GROUP


def remote(src, dst, send, recv, b, r):
    return pltpu.make_async_remote_copy(
        src_ref=src, dst_ref=dst, send_sem=send, recv_sem=recv, device_id=(b, r), device_id_type=MESH
    )


def greet(peers):
    barrier = pltpu.get_barrier_semaphore()
    for peer in peers:
        pl.semaphore_signal(barrier, inc=1, device_id=peer, device_id_type=MESH)
    pl.semaphore_wait(barrier, len(peers))


def columns(ref, block):
    return ref.at[:, :, pl.ds(pl.multiple_of(block * TILE, TILE), TILE)]


def forward_kernel(
    nb, run,
    feats, weight, vals, table, cot,
    out, wterm, bt_all, vals_all, table_all,
    win, vbuf, tbuf, tsm, wv, cv, ov, aggs, aggr, slope, bts, wt,
    fs, fr, us, ur, ds_, dr, us2, ur2, ds2, dr2, vs, vr, ts, tr, asend, arecv, bsend, brecv, loc,
):
    b, r, flip, g, up, down, r_up, r_down, p1, p2, p3 = place(nb, run)
    greet([(b, p1), (b, p2), (b, p3), (up, r_up), (down, r_down)])

    def group_of(member):
        return (member + flip) % GROUP

    sends = []

    def go(copy):
        copy.start()
        sends.append(copy)

    rows = vals.shape[0]
    panel_blocks = GROUP * rows
    dead = SPAN * panel_blocks

    def piece(panel, member):
        return win.at[pl.ds(panel * panel_blocks + member * rows, rows)]

    mine = columns(feats, g)
    for slot, p in ((0, p2), (1, p3), (2, p1)):
        go(remote(columns(feats, group_of(p)), piece(2, r), fs.at[slot], fr.at[r], b, p))
    go(remote(mine, piece(1, r), us.at[0], ur.at[r], up, r_up))
    go(remote(mine, piece(3, r), ds_.at[0], dr.at[r], down, r_down))
    for slot, p in ((0, p2), (1, p3), (2, p1)):
        go(remote(table, tbuf.at[r], ts.at[slot], tr.at[r], b, p))
    for c in range(rows):
        go(remote(vals.at[c], vbuf.at[r, c], vs.at[0, c], vr.at[r, c], b, p2))
        go(remote(vals.at[c], vbuf.at[r, c], vs.at[1, c], vr.at[r, c], b, p1))
    own = [
        pltpu.make_async_copy(mine, piece(2, r), loc.at[0]),
        pltpu.make_async_copy(vals, vbuf.at[r], loc.at[1]),
        pltpu.make_async_copy(table, tbuf.at[r], loc.at[2]),
        pltpu.make_async_copy(weight, wv, loc.at[3]),
        pltpu.make_async_copy(cot, cv, loc.at[4]),
    ]
    for copy in own:
        copy.start()
    win[dead] = jnp.zeros((TILE, TILE), BF16)

    def landed(dst, recv):
        remote(dst, dst, fs.at[0], recv, b, p1).wait_recv()

    for slot, p in ((1, p1), (2, p2), (3, p3)):
        landed(piece(2, p), fr.at[p])
        go(remote(piece(2, p), piece(1, p), us.at[slot], ur.at[p], up, r_up))
        go(remote(piece(2, p), piece(3, p), ds_.at[slot], dr.at[p], down, r_down))
    from_below = partners(r_down)
    from_above = partners(r_up)
    for slot in range(GROUP):
        i = from_below[slot]
        landed(piece(1, i), ur.at[i])
        go(remote(piece(1, i), piece(0, i), us2.at[slot], ur2.at[i], up, r_up))
        i = from_above[slot]
        landed(piece(3, i), dr.at[i])
        go(remote(piece(3, i), piece(4, i), ds2.at[slot], dr2.at[i], down, r_down))
        if slot < rows:
            landed(vbuf.at[p2, slot], vr.at[p2, slot])
            go(remote(vbuf.at[p2, slot], vbuf.at[p2, slot], vs.at[2, slot], vr.at[p2, slot], b, p1))
    for i in range(GROUP):
        landed(piece(0, i), ur2.at[i])
        landed(piece(4, i), dr2.at[i])
    for p in (p1, p3):
        for c in range(rows):
            landed(vbuf.at[p, c], vr.at[p, c])
    for p in (p1, p2, p3):
        landed(tbuf.at[p], tr.at[p])
    for copy in own:
        copy.wait()
    to_scalars = pltpu.make_async_copy(tbuf, tsm, loc.at[0])
    to_scalars.start()
    keep = [
        pltpu.make_async_copy(vbuf, vals_all, loc.at[1]),
        pltpu.make_async_copy(tbuf, table_all, loc.at[2]),
    ]
    for copy in keep:
        copy.start()
    to_scalars.wait()

    for slot, q in ((0, p2), (1, p3), (2, p1), (3, r)):

        def one_row(kk, carry, q=q):
            left = [vbuf[q, kk, s] for s in range(SLOTS)]
            right = [win[tsm[q, 0, kk * SLOTS + s]] for s in range(SLOTS)]
            total = jnp.dot(
                jnp.concatenate(left, axis=1), jnp.concatenate(right, axis=0), preferred_element_type=F32
            )
            aggs[q, pl.ds(pl.multiple_of(kk * TILE, TILE), TILE), :] = total.astype(BF16)
            return carry

        lax.fori_loop(0, rows, one_row, 0)
        if slot < 3:
            go(remote(aggs.at[q], aggr.at[g], asend.at[slot], arecv.at[g], b, q))
        else:
            last = pltpu.make_async_copy(aggs.at[q], aggr.at[g], loc.at[0])
            last.start()
            last.wait()
    for p in (p1, p2, p3):
        gp = group_of(p)
        landed(aggr.at[gp], arecv.at[gp])

    def dense(t, carry):
        span = pl.ds(pl.multiple_of(t * TILE, TILE), TILE)
        agg = jnp.concatenate([aggr[i, span, :] for i in range(GROUP)], axis=1)
        pre = jnp.dot(agg, wv[...], preferred_element_type=F32)
        sigma = jax.nn.sigmoid(pre)
        ov[span, :] = (pre * sigma).astype(BF16)
        grad = cv[span, :].astype(F32) * (sigma * (1.0 + pre * (1.0 - sigma)))
        slope[span, :] = grad.astype(BF16)
        return carry

    lax.fori_loop(0, rows, dense, 0)
    tail = [pltpu.make_async_copy(ov, out, loc.at[3])]
    tail[0].start()
    for slot, q in ((0, p2), (1, p3), (2, p1), (3, r)):
        gq = group_of(q)
        part = wv[pl.ds(pl.multiple_of(gq * TILE, TILE), TILE), :]
        back = lax.dot_general(part, slope[...], (((1,), (1,)), ((), ())), preferred_element_type=F32)
        bts[q] = back.astype(BF16)
        if slot < 3:
            go(remote(bts.at[q], bt_all.at[r], bsend.at[slot], brecv.at[r], b, q))
        else:
            copy = pltpu.make_async_copy(bts.at[q], bt_all.at[r], loc.at[4])
            copy.start()
            tail.append(copy)
    for i in range(GROUP):
        wt[pl.ds(i * TILE, TILE), :] = lax.dot_general(
            aggr[i], slope[...], (((0,), (0,)), ((), ())), preferred_element_type=F32
        )
    copy = pltpu.make_async_copy(wt, wterm, loc.at[0])
    copy.start()
    tail.append(copy)
    for copy in keep + tail:
        copy.wait()
    for p in (p1, p2, p3):
        landed(bt_all.at[p], brecv.at[p])
    for copy in sends:
        copy.wait_send()


def scatter_kernel(rows, table, vals, bt, near, far, acc):
    k = pl.program_id(0)
    panel_blocks = GROUP * rows

    @pl.when(k == 0)
    def _():
        acc[...] = jnp.zeros_like(acc)

    tiles = jnp.concatenate([vals[0, 0, s] for s in range(SLOTS)], axis=1)
    terms = jnp.dot(bt[0], tiles, preferred_element_type=F32)
    for s in range(SLOTS):
        index = table[k // rows, 0, (k % rows) * SLOTS + s]
        acc[index] += terms[:, s * TILE : (s + 1) * TILE]

    @pl.when(k == panel_blocks - 1)
    def _():
        near[...] = acc[pl.ds(panel_blocks, 3 * panel_blocks)]
        far[0] = acc[pl.ds(0, panel_blocks)].astype(BF16)
        far[1] = acc[pl.ds(4 * panel_blocks, panel_blocks)].astype(BF16)


def return_kernel(
    nb, run, scale,
    near, far, wterm,
    grad, wgrad,
    ru2, rd2, su, sd, ru1, rd1, tot, rt, gv, a1, s1, a2, s2, a3, b3, b2, b1, wv,
    us, ur, ds_, dr, us2, ur2, ds2, dr2, ts, tr, w1s, w1r, w2s, w2r, w3s, w3r, x3s, x3r, x2s, x2r, x1s, x1r, loc,
):
    b, r, flip, g, up, down, r_up, r_down, p1, p2, p3 = place(nb, run)
    runs = nb // run
    m, z = b // run, b % run
    across = [((m + i) % runs) for i in range(1, runs)]
    along = [((z + i) % run) for i in range(1, run)]
    panel_peers = (p1, p2, p3)
    greet(
        [(b, p) for p in panel_peers]
        + [(up, r_up), (down, r_down)]
        + [(i * run + z, r) for i in across]
        + [(m * run + i, r) for i in along]
    )
    rows = gv.shape[0] // TILE
    sends = []

    def go(copy):
        copy.start()
        sends.append(copy)

    def landed(dst, recv):
        remote(dst, dst, ts.at[0], recv, b, p1).wait_recv()

    order = (p2, p3, p1, r)
    for slot, q in enumerate(order):
        block = pl.ds(q * rows, rows)
        go(remote(far.at[1, block], ru2.at[q], us.at[slot], ur.at[q], up, r_up))
        go(remote(far.at[0, block], rd2.at[q], ds_.at[slot], dr.at[q], down, r_down))
    quarter = wterm.shape[0] // GROUP
    for slot, q in enumerate((p2, p3, p1)):
        part = wterm.at[pl.ds(pl.multiple_of(q * quarter, quarter), quarter), :]
        go(remote(part, a1.at[r], w1s.at[slot], w1r.at[r], b, q))

    def relay(slot):
        q = partners_down[slot]
        landed(ru2.at[q], ur.at[q])
        su[q] = (ru2[q].astype(F32) + near[2, pl.ds(q * rows, rows)]).astype(BF16)
        go(remote(su.at[q], ru1.at[q], us2.at[slot], ur2.at[q], up, r_up))
        q = partners_up[slot]
        landed(rd2.at[q], dr.at[q])
        sd[q] = (rd2[q].astype(F32) + near[0, pl.ds(q * rows, rows)]).astype(BF16)
        go(remote(sd.at[q], rd1.at[q], ds2.at[slot], dr2.at[q], down, r_down))

    def ordered(member):
        a, c, d, e = partners(member)
        return d, e, c, a

    partners_down = ordered(r_down)
    partners_up = ordered(r_up)

    def finish(slot):
        q = order[slot]
        landed(ru1.at[q], ur2.at[q])
        landed(rd1.at[q], dr2.at[q])
        total = near[1, pl.ds(q * rows, rows)] + ru1[q].astype(F32) + rd1[q].astype(F32)
        tot[q] = total.astype(BF16)
        if slot < 3:
            go(remote(tot.at[q], rt.at[g], ts.at[slot], tr.at[g], b, q))
        else:
            rt[g] = tot[q]

    for slot in range(GROUP):
        relay(slot)
    for p in panel_peers:
        landed(a1.at[p], w1r.at[p])
    s1[...] = wterm[pl.ds(pl.multiple_of(r * quarter, quarter), quarter), :] + a1[p1] + (a1[p2] + a1[p3])
    piece = quarter // runs
    for slot, i in enumerate(across):
        part = s1.at[pl.ds(pl.multiple_of(i * piece, piece), piece), :]
        go(remote(part, a2.at[m], w2s.at[slot], w2r.at[m], i * run + z, r))
    finish(0)
    for i in across:
        landed(a2.at[i], w2r.at[i])
    total = s1[pl.ds(pl.multiple_of(m * piece, piece), piece), :]
    for i in across:
        total = total + a2[i]
    s2[...] = total
    tall = piece // (run // 4)

    def corner(ref, i):
        return ref.at[pl.ds(pl.multiple_of((i // 4) * tall, tall), tall), pl.ds(pl.multiple_of((i % 4) * TILE, TILE), TILE)]

    for slot, i in enumerate(along):
        go(remote(corner(s2, i), a3.at[z], w3s.at[slot], w3r.at[z], m * run + i, r))
    finish(1)
    for i in along:
        landed(a3.at[i], w3r.at[i])
    total = corner(s2, z)[...]
    for i in along:
        total = total + a3[i]
    corner(b3, z)[...] = total * scale
    for slot, i in enumerate(along):
        go(remote(corner(b3, z), corner(b3, z), x3s.at[slot], x3r.at[z], m * run + i, r))
    finish(2)
    for i in along:
        landed(corner(b3, i), x3r.at[i])
    b2[m] = b3[...].astype(BF16)
    for slot, i in enumerate(across):
        go(remote(b2.at[m], b2.at[m], x2s.at[slot], x2r.at[m], i * run + z, r))
    finish(3)
    for i in across:
        landed(b2.at[i], x2r.at[i])
    for slot, q in enumerate((p2, p3, p1)):
        go(remote(b2, b1.at[r], x1s.at[slot], x1r.at[r], b, q))
    b1[r] = b2[...]

    eye = (
        lax.broadcasted_iota(jnp.int32, (TILE, TILE), 0) == lax.broadcasted_iota(jnp.int32, (TILE, TILE), 1)
    ).astype(BF16)
    for p in panel_peers:
        gp = (p + flip) % GROUP
        landed(rt.at[gp], tr.at[gp])
    for i in range(GROUP):
        for t in range(rows):
            turned = lax.dot_general(eye, rt[i, t], (((1,), (1,)), ((), ())), preferred_element_type=F32)
            gv[pl.ds(t * TILE, TILE), pl.ds(i * TILE, TILE)] = turned.astype(BF16)
    done = pltpu.make_async_copy(gv, grad, loc.at[0])
    done.start()
    for p in panel_peers:
        landed(b1.at[p], x1r.at[p])
    for i in range(GROUP):
        for j in range(runs):
            wv[pl.ds(i * quarter + j * piece, piece), :] = b1[i, j].astype(F32)
    copy = pltpu.make_async_copy(wv, wgrad, loc.at[1])
    copy.start()
    done.wait()
    copy.wait()
    for copy in sends:
        copy.wait_send()


def window_table(tile_cols, tile_count, panel_blocks, nb):
    center = lax.axis_index("blk")
    offset = (tile_cols // panel_blocks - center) % nb
    offset = jnp.where(offset > REACH, offset - nb, offset)
    index = (offset + REACH) * panel_blocks + tile_cols % panel_blocks
    dead = SPAN * panel_blocks
    alive = jnp.arange(SLOTS, dtype=jnp.int32)[None, :] < tile_count[:, None]
    index = jnp.where(alive, jnp.clip(index, 0, dead - 1), dead).astype(jnp.int32)
    flat = index.reshape(1, -1)
    return jnp.pad(flat, ((0, 7), (0, TILE - flat.shape[1])))


def local(nb, run, feats, weight, vals, cols, count, cot):
    nodes, width = feats.shape
    rows = nodes // TILE
    panel_blocks = GROUP * rows
    runs = nb // run
    table = window_table(cols, count, panel_blocks, nb)
    anywhere = pl.BlockSpec(memory_space=pl.ANY)
    dma = pltpu.SemaphoreType.DMA
    shape = jax.ShapeDtypeStruct
    out, wterm, bt, vals_all, table_all = pl.pallas_call(
        functools.partial(forward_kernel, nb, run),
        out_shape=(
            shape((nodes, width), BF16),
            shape((width, width), F32),
            shape((GROUP, TILE, nodes), BF16),
            shape((GROUP, rows, SLOTS, TILE, TILE), BF16),
            shape((GROUP, 8, TILE), jnp.int32),
        ),
        in_specs=[anywhere] * 5,
        out_specs=(anywhere,) * 5,
        scratch_shapes=[
            pltpu.VMEM((SPAN * panel_blocks + 1, TILE, TILE), BF16),
            pltpu.VMEM((GROUP, rows, SLOTS, TILE, TILE), BF16),
            pltpu.VMEM((GROUP, 8, TILE), jnp.int32),
            pltpu.SMEM((GROUP, 8, TILE), jnp.int32),
            pltpu.VMEM((width, width), BF16),
            pltpu.VMEM((nodes, width), BF16),
            pltpu.VMEM((nodes, width), BF16),
            pltpu.VMEM((GROUP, nodes, TILE), BF16),
            pltpu.VMEM((GROUP, nodes, TILE), BF16),
            pltpu.VMEM((nodes, width), BF16),
            pltpu.VMEM((GROUP, TILE, nodes), BF16),
            pltpu.VMEM((width, width), F32),
            dma((3,)), dma((GROUP,)),
            dma((GROUP,)), dma((GROUP,)), dma((GROUP,)), dma((GROUP,)),
            dma((GROUP,)), dma((GROUP,)), dma((GROUP,)), dma((GROUP,)),
            dma((3, rows)), dma((GROUP, rows)),
            dma((3,)), dma((GROUP,)),
            dma((3,)), dma((GROUP,)),
            dma((3,)), dma((GROUP,)),
            dma((5,)),
        ],
        compiler_params=pltpu.CompilerParams(
            collective_id=0, has_side_effects=True, vmem_limit_bytes=60 << 20
        ),
        name="forward",
    )(feats.reshape(rows, TILE, width), weight, vals, table, cot)

    near, far = pl.pallas_call(
        functools.partial(scatter_kernel, rows),
        grid_spec=pltpu.PrefetchScalarGridSpec(
            num_scalar_prefetch=1,
            grid=(panel_blocks,),
            in_specs=[
                pl.BlockSpec((1, 1, SLOTS, TILE, TILE), lambda k, t: (k // rows, k % rows, 0, 0, 0)),
                pl.BlockSpec((1, TILE, TILE), lambda k, t: (k // rows, 0, k % rows)),
            ],
            out_specs=(
                pl.BlockSpec((3 * panel_blocks, TILE, TILE), lambda k, t: (0, 0, 0)),
                pl.BlockSpec((2, panel_blocks, TILE, TILE), lambda k, t: (0, 0, 0, 0)),
            ),
            scratch_shapes=[pltpu.VMEM((SPAN * panel_blocks + 1, TILE, TILE), F32)],
        ),
        out_shape=(
            shape((3 * panel_blocks, TILE, TILE), F32),
            shape((2, panel_blocks, TILE, TILE), BF16),
        ),
        compiler_params=pltpu.CompilerParams(
            dimension_semantics=("arbitrary",), vmem_limit_bytes=48 << 20
        ),
        name="scatter",
    )(table_all, vals_all, bt)

    chunk = (GROUP, rows, TILE, TILE)
    quarter = width // GROUP
    piece = quarter // runs
    tall = piece // (run // 4)
    in_vmem = pl.BlockSpec(memory_space=pltpu.VMEM)
    grad, wgrad = pl.pallas_call(
        functools.partial(return_kernel, nb, run, 1.0 / math.sqrt(nodes * GROUP * nb)),
        out_shape=(shape((nodes, width), BF16), shape((width, width), F32)),
        in_specs=[in_vmem, in_vmem, in_vmem],
        out_specs=(anywhere, anywhere),
        scratch_shapes=[
            pltpu.VMEM(chunk, BF16), pltpu.VMEM(chunk, BF16),
            pltpu.VMEM(chunk, BF16), pltpu.VMEM(chunk, BF16),
            pltpu.VMEM(chunk, BF16), pltpu.VMEM(chunk, BF16),
            pltpu.VMEM(chunk, BF16), pltpu.VMEM(chunk, BF16),
            pltpu.VMEM((nodes, width), BF16),
            pltpu.VMEM((GROUP, quarter, width), F32),
            pltpu.VMEM((quarter, width), F32),
            pltpu.VMEM((runs, piece, width), F32),
            pltpu.VMEM((piece, width), F32),
            pltpu.VMEM((run, tall, TILE), F32),
            pltpu.VMEM((piece, width), F32),
            pltpu.VMEM((runs, piece, width), BF16),
            pltpu.VMEM((GROUP, runs, piece, width), BF16),
            pltpu.VMEM((width, width), F32),
        ]
        + [dma((GROUP,))] * 10
        + [dma((3,)), dma((GROUP,))]
        + [dma((runs,)), dma((runs,))]
        + [dma((run,)), dma((run,))]
        + [dma((run,)), dma((run,))]
        + [dma((runs,)), dma((runs,))]
        + [dma((3,)), dma((GROUP,))]
        + [dma((2,))],
        compiler_params=pltpu.CompilerParams(
            collective_id=1, has_side_effects=True, vmem_limit_bytes=48 << 20
        ),
        name="giveback",
    )(near.reshape(3, panel_blocks, TILE, TILE), far, wterm)
    return out, wgrad, grad


def solution(mesh, run=RUN):
    both = ("blk", "repl")
    in_specs = (
        P(both, None),
        P(),
        P(both, None, None, None),
        P(both, None),
        P(both),
        P(both, None),
    )
    out_specs = (P(both, None), P(), P(both, None))
    body = functools.partial(local, mesh.shape["blk"], run)
    return jax.shard_map(body, mesh=mesh, in_specs=in_specs, out_specs=out_specs, check_vma=False)
```

```python
import functools
import math

import jax
import jax.numpy as jnp
from jax import lax
from jax.experimental import pallas as pl
from jax.experimental.pallas import tpu as pltpu
from jax.sharding import PartitionSpec as P

TILE = 128
SLOTS = 8
REACH = 2
SPAN = 2 * REACH + 1
GROUP = 4
MESH = pl.DeviceIdType.MESH
BF16 = jnp.bfloat16
F32 = jnp.float32
RUN = 8


def place(nb, run):
    b = lax.axis_index("blk")
    r = lax.axis_index("repl")
    flip = 2 * ((b // run) % 2)
    g = (r + flip) % GROUP
    up = (b + 1) % nb
    down = (b + nb - 1) % nb
    r_up = (g + 2 * ((up // run) % 2)) % GROUP
    r_down = (g + 2 * ((down // run) % 2)) % GROUP
    p1 = r + 1 - 2 * (r % 2)
    p2 = (r + 2) % GROUP
    p3 = (p1 + 2) % GROUP
    return b, r, flip, g, up, down, r_up, r_down, p1, p2, p3


def partners(r):
    p1 = r + 1 - 2 * (r % 2)
    return r, p1, (r + 2) % GROUP, (p1 + 2) % GROUP


def remote(src, dst, send, recv, b, r):
    return pltpu.make_async_remote_copy(
        src_ref=src, dst_ref=dst, send_sem=send, recv_sem=recv, device_id=(b, r), device_id_type=MESH
    )


def greet(peers):
    barrier = pltpu.get_barrier_semaphore()
    for peer in peers:
        pl.semaphore_signal(barrier, inc=1, device_id=peer, device_id_type=MESH)
    pl.semaphore_wait(barrier, len(peers))


def ordered(member):
    own, core, chip, both = partners(member)
    return chip, both, core, own


def columns(ref, block):
    return ref.at[:, :, pl.ds(pl.multiple_of(block * TILE, TILE), TILE)]


def sorted_entries(dest):
    rows = lax.broadcasted_iota(jnp.int32, (TILE, TILE), 0)
    lanes = lax.broadcasted_iota(jnp.int32, (TILE, TILE), 1)
    across = jnp.broadcast_to(dest, (TILE, TILE))

    def count(mask, axis, value=1):
        return jnp.sum(jnp.where(mask, value, 0), axis=axis, keepdims=True)

    down = jnp.broadcast_to(count(rows == lanes, 1, across), (TILE, TILE))
    tie = (across == down) & (lanes < rows)
    rank = jnp.broadcast_to(count((across < down) | tie, 1), (TILE, TILE))
    repeat = jnp.broadcast_to(count(tie, 1), (TILE, TILE)) > 0
    hit = rank == lanes
    order = count(hit, 0, rows)
    before = jnp.where(count(hit & repeat, 0) > 0, lanes[0:1, :] - 1, TILE)
    owner = count(hit, 0, rows // SLOTS)
    upto = count(down <= lanes, 0)
    last = jnp.where(count(down == lanes, 0) > 0, upto - 1, TILE)
    return order, before, owner, last


def layer_kernel(
    nb, run, scale,
    feats, weight, vals, table, cot,
    out, grad, wgrad,
    win, vbuf, tbuf, smv, tsm, wv, cv, ov, aggs, aggr, slope, bts, btp, wt, runs,
    far, su, sd, ru2, rd2, ru1, rd1, tot, rt, gv, a1, s1, a2, s2, a3, b3, b2, b1, gw,
    fs, fr, us, ur, ds_, dr, us2, ur2, ds2, dr2, vs, vr, ts, tr, asend, arecv, bsend, brecv,
    vus, vur, vds, vdr, vus2, vur2, vds2, vdr2, gs, gr,
    w1s, w1r, w2s, w2r, w3s, w3r, x3s, x3r, x2s, x2r, x1s, x1r, loc,
):
    b, r, flip, g, up, down, r_up, r_down, p1, p2, p3 = place(nb, run)
    lines = nb // run
    m, z = b // run, b % run
    across = [((m + i) % lines) for i in range(1, lines)]
    along = [((z + i) % run) for i in range(1, run)]
    panel_peers = (p1, p2, p3)
    order = (p2, p3, p1, r)
    greet(
        [(b, p) for p in panel_peers]
        + [(up, r_up), (down, r_down)]
        + [(i * run + z, r) for i in across]
        + [(m * run + i, r) for i in along]
    )

    def group_of(member):
        return (member + flip) % GROUP

    sends = []

    def go(copy):
        copy.start()
        sends.append(copy)

    def landed(dst, recv):
        remote(dst, dst, fs.at[0], recv, b, p1).wait_recv()

    rows = vals.shape[0]
    panel_blocks = GROUP * rows
    dead = SPAN * panel_blocks

    def piece(panel, member):
        return win.at[pl.ds(panel * panel_blocks + member * rows, rows)]

    def tiles(member, c):
        return vbuf.at[pl.ds((member * rows + c) * SLOTS, SLOTS)]

    mine = columns(feats, g)
    for slot, p in enumerate((p2, p3, p1)):
        go(remote(columns(feats, group_of(p)), piece(2, r), fs.at[slot], fr.at[r], b, p))
    go(remote(mine, piece(1, r), us.at[0], ur.at[r], up, r_up))
    go(remote(mine, piece(3, r), ds_.at[0], dr.at[r], down, r_down))
    for slot, p in enumerate((p2, p3, p1)):
        go(remote(table, tbuf.at[r], ts.at[slot], tr.at[r], b, p))
    for c in range(rows):
        go(remote(vals.at[c], tiles(r, c), vs.at[0, c], vr.at[r, c], b, p2))
        go(remote(vals.at[c], tiles(r, c), vs.at[1, c], vr.at[r, c], b, p1))
    own = [
        pltpu.make_async_copy(table, tbuf.at[r], loc.at[0]),
        pltpu.make_async_copy(mine, piece(2, r), loc.at[1]),
        pltpu.make_async_copy(weight, wv, loc.at[2]),
        pltpu.make_async_copy(cot, cv, loc.at[3]),
    ] + [pltpu.make_async_copy(vals.at[c], tiles(r, c), loc.at[4 + c]) for c in range(rows)]
    for copy in own:
        copy.start()
    win[dead] = jnp.zeros((TILE, TILE), BF16)
    runs[TILE] = jnp.zeros((TILE, TILE), F32)

    for slot, p in ((1, p1), (2, p2), (3, p3)):
        landed(piece(2, p), fr.at[p])
        go(remote(piece(2, p), piece(1, p), us.at[slot], ur.at[p], up, r_up))
        go(remote(piece(2, p), piece(3, p), ds_.at[slot], dr.at[p], down, r_down))
    for p in panel_peers:
        landed(tbuf.at[p], tr.at[p])
    own[0].wait()
    dest = (tbuf[0] + tbuf[1]) + (tbuf[2] + tbuf[3])
    smv[0] = dest
    for line, value in enumerate(sorted_entries(dest[0:1, :])):
        smv[line + 1] = jnp.broadcast_to(value, (8, TILE))
    to_scalars = pltpu.make_async_copy(smv, tsm, loc.at[0])
    to_scalars.start()

    from_below = partners(r_down)
    from_above = partners(r_up)
    for slot in range(GROUP):
        i = from_below[slot]
        landed(piece(1, i), ur.at[i])
        go(remote(piece(1, i), piece(0, i), us2.at[slot], ur2.at[i], up, r_up))
        i = from_above[slot]
        landed(piece(3, i), dr.at[i])
        go(remote(piece(3, i), piece(4, i), ds2.at[slot], dr2.at[i], down, r_down))
        if slot < rows:
            landed(tiles(p2, slot), vr.at[p2, slot])
            go(remote(tiles(p2, slot), tiles(p2, slot), vs.at[2, slot], vr.at[p2, slot], b, p1))
    for i in range(GROUP):
        landed(piece(0, i), ur2.at[i])
        landed(piece(4, i), dr2.at[i])
    for copy in own[1:]:
        copy.wait()
    to_scalars.wait()
    for p in (p1, p3):
        for c in range(rows):
            landed(tiles(p, c), vr.at[p, c])

    for slot, q in enumerate(order):

        def one_row(kk, carry, q=q):
            first = (q * rows + kk) * SLOTS
            left = [vbuf[first + s] for s in range(SLOTS)]
            right = [win[tsm[0, 0, first + s]] for s in range(SLOTS)]
            total = jnp.dot(
                jnp.concatenate(left, axis=1), jnp.concatenate(right, axis=0), preferred_element_type=F32
            )
            aggs[q, pl.ds(pl.multiple_of(kk * TILE, TILE), TILE), :] = total.astype(BF16)
            return carry

        lax.fori_loop(0, rows, one_row, 0)
        if slot < 3:
            go(remote(aggs.at[q], aggr.at[g], asend.at[slot], arecv.at[g], b, q))
        else:
            last = pltpu.make_async_copy(aggs.at[q], aggr.at[g], loc.at[0])
            last.start()
            last.wait()
    for p in panel_peers:
        gp = group_of(p)
        landed(aggr.at[gp], arecv.at[gp])

    def dense(t, carry):
        span = pl.ds(pl.multiple_of(t * TILE, TILE), TILE)
        agg = jnp.concatenate([aggr[i, span, :] for i in range(GROUP)], axis=1)
        pre = jnp.dot(agg, wv[...], preferred_element_type=F32)
        sigma = jax.nn.sigmoid(pre)
        ov[span, :] = (pre * sigma).astype(BF16)
        slant = cv[span, :].astype(F32) * (sigma * (1.0 + pre * (1.0 - sigma)))
        slope[span, :] = slant.astype(BF16)
        return carry

    lax.fori_loop(0, rows, dense, 0)
    ends = [pltpu.make_async_copy(ov, out, loc.at[1])]
    ends[0].start()

    def back_rows(q):
        part = wv[pl.ds(pl.multiple_of(group_of(q) * TILE, TILE), TILE), :]
        for t in range(rows):
            turned = lax.dot_general(
                part, slope[pl.ds(t * TILE, TILE), :], (((1,), (1,)), ((), ())), preferred_element_type=F32
            )
            yield t, turned.astype(BF16)

    for slot, q in enumerate(order):
        for t, value in back_rows(q):
            if slot < 3:
                bts[slot, t] = value
            else:
                btp[r * rows + t] = value
        if slot < 3:
            go(remote(bts.at[slot], btp.at[pl.ds(r * rows, rows)], bsend.at[slot], brecv.at[r], b, q))
    for slot, q in enumerate(order):
        wt[q] = lax.dot_general(aggr[q], slope[...], (((0,), (0,)), ((), ())), preferred_element_type=F32)
        if slot < 3:
            go(remote(wt.at[q], a1.at[r], w1s.at[slot], w1r.at[r], b, q))
    for p in panel_peers:
        landed(btp.at[pl.ds(p * rows, rows)], brecv.at[p])

    def eight(t, carry):
        first = t * 8
        terms = [
            jnp.dot(btp[tsm[3, 0, first + i]], vbuf[tsm[1, 0, first + i]], preferred_element_type=F32)
            for i in range(8)
        ]
        for i in range(8):
            runs[first + i] = terms[i] + runs[tsm[2, 0, first + i]]
        return carry

    lax.fori_loop(0, panel_blocks * SLOTS // 8, eight, 0)

    def share(panel, q, t):
        return runs[tsm[4, 0, panel * panel_blocks + q * rows + t]]

    for slot, q in enumerate(order):
        for t in range(rows):
            far[0, q, t] = share(4, q, t).astype(BF16)
            far[1, q, t] = share(0, q, t).astype(BF16)
        go(remote(far.at[0, q], ru2.at[q], vus.at[slot], vur.at[q], up, r_up))
        go(remote(far.at[1, q], rd2.at[q], vds.at[slot], vdr.at[q], down, r_down))

    order_below = ordered(r_down)
    order_above = ordered(r_up)

    def relay(slot):
        q = order_below[slot]
        landed(ru2.at[q], vur.at[q])
        for t in range(rows):
            su[q, t] = (ru2[q, t].astype(F32) + share(3, q, t)).astype(BF16)
        go(remote(su.at[q], ru1.at[q], vus2.at[slot], vur2.at[q], up, r_up))
        q = order_above[slot]
        landed(rd2.at[q], vdr.at[q])
        for t in range(rows):
            sd[q, t] = (rd2[q, t].astype(F32) + share(1, q, t)).astype(BF16)
        go(remote(sd.at[q], rd1.at[q], vds2.at[slot], vdr2.at[q], down, r_down))

    def finish(slot):
        q = order[slot]
        landed(ru1.at[q], vur2.at[q])
        landed(rd1.at[q], vdr2.at[q])
        for t in range(rows):
            total = share(2, q, t) + (ru1[q, t].astype(F32) + rd1[q, t].astype(F32))
            if slot < 3:
                tot[q, t] = total.astype(BF16)
            else:
                rt[g, t] = total.astype(BF16)
        if slot < 3:
            go(remote(tot.at[q], rt.at[g], gs.at[slot], gr.at[g], b, q))

    quarter = wt.shape[1]
    part = quarter // lines
    tall = part // (run // 4)

    def corner(ref, i):
        return ref.at[pl.ds(pl.multiple_of((i // 4) * tall, tall), tall), pl.ds(pl.multiple_of((i % 4) * TILE, TILE), TILE)]

    relay(0)
    relay(1)
    for p in panel_peers:
        landed(a1.at[p], w1r.at[p])
    s1[...] = wt[r] + a1[p1] + (a1[p2] + a1[p3])
    for slot, i in enumerate(across):
        chunk = s1.at[pl.ds(pl.multiple_of(i * part, part), part), :]
        go(remote(chunk, a2.at[m], w2s.at[slot], w2r.at[m], i * run + z, r))
    relay(2)
    relay(3)
    for i in across:
        landed(a2.at[i], w2r.at[i])
    total = s1[pl.ds(pl.multiple_of(m * part, part), part), :]
    for i in across:
        total = total + a2[i]
    s2[...] = total
    for slot, i in enumerate(along):
        go(remote(corner(s2, i), a3.at[z], w3s.at[slot], w3r.at[z], m * run + i, r))
    finish(0)
    for i in along:
        landed(a3.at[i], w3r.at[i])
    total = corner(s2, z)[...]
    for i in along:
        total = total + a3[i]
    corner(b3, z)[...] = total * scale
    for slot, i in enumerate(along):
        go(remote(corner(b3, z), corner(b3, z), x3s.at[slot], x3r.at[z], m * run + i, r))
    finish(1)
    for i in along:
        landed(corner(b3, i), x3r.at[i])
    b2[m] = b3[...].astype(BF16)
    for slot, i in enumerate(across):
        go(remote(b2.at[m], b2.at[m], x2s.at[slot], x2r.at[m], i * run + z, r))
    finish(2)
    for i in across:
        landed(b2.at[i], x2r.at[i])
    for slot, q in enumerate((p2, p3, p1)):
        go(remote(b2, b1.at[r], x1s.at[slot], x1r.at[r], b, q))
    b1[r] = b2[...]
    finish(3)

    eye = (
        lax.broadcasted_iota(jnp.int32, (TILE, TILE), 0) == lax.broadcasted_iota(jnp.int32, (TILE, TILE), 1)
    ).astype(BF16)
    for p in panel_peers:
        gp = group_of(p)
        landed(rt.at[gp], gr.at[gp])
    for i in range(GROUP):
        for t in range(rows):
            turned = lax.dot_general(eye, rt[i, t], (((1,), (1,)), ((), ())), preferred_element_type=F32)
            gv[pl.ds(t * TILE, TILE), pl.ds(i * TILE, TILE)] = turned.astype(BF16)
    ends.append(pltpu.make_async_copy(gv, grad, loc.at[2]))
    ends[-1].start()
    for p in panel_peers:
        landed(b1.at[p], x1r.at[p])
    for i in range(GROUP):
        for j in range(lines):
            gw[pl.ds(i * quarter + j * part, part), :] = b1[i, j].astype(F32)
    ends.append(pltpu.make_async_copy(gw, wgrad, loc.at[3]))
    ends[-1].start()
    for copy in ends:
        copy.wait()
    for copy in sends:
        copy.wait_send()


def window_table(tile_cols, tile_count, panel_blocks, nb):
    center = lax.axis_index("blk")
    offset = (tile_cols // panel_blocks - center) % nb
    offset = jnp.where(offset > REACH, offset - nb, offset)
    index = (offset + REACH) * panel_blocks + tile_cols % panel_blocks
    dead = SPAN * panel_blocks
    alive = jnp.arange(SLOTS, dtype=jnp.int32)[None, :] < tile_count[:, None]
    index = jnp.where(alive, jnp.clip(index, 0, dead - 1), dead).astype(jnp.int32)
    line = jnp.tile(index.reshape(1, -1), (8, GROUP))
    lane = lax.broadcasted_iota(jnp.int32, line.shape, 1)
    return jnp.where(lane // index.size == lax.axis_index("repl"), line, 0)


def local(nb, run, feats, weight, vals, cols, count, cot):
    nodes, width = feats.shape
    rows = nodes // TILE
    panel_blocks = GROUP * rows
    lines = nb // run
    table = window_table(cols, count, panel_blocks, nb)
    anywhere = pl.BlockSpec(memory_space=pl.ANY)
    dma = pltpu.SemaphoreType.DMA
    shape = jax.ShapeDtypeStruct
    chunk = (GROUP, rows, TILE, TILE)
    quarter = width // GROUP
    part = quarter // lines
    tall = part // (run // 4)
    pair = [dma((GROUP,)), dma((GROUP,))]
    out, grad, wgrad = pl.pallas_call(
        functools.partial(layer_kernel, nb, run, 1.0 / math.sqrt(nodes * GROUP * nb)),
        out_shape=(
            shape((nodes, width), BF16),
            shape((nodes, width), BF16),
            shape((width, width), F32),
        ),
        in_specs=[anywhere] * 5,
        out_specs=(anywhere,) * 3,
        scratch_shapes=[
            pltpu.VMEM((SPAN * panel_blocks + 1, TILE, TILE), BF16),
            pltpu.VMEM((panel_blocks * SLOTS, TILE, TILE), BF16),
            pltpu.VMEM((GROUP, 8, TILE), jnp.int32),
            pltpu.VMEM((5, 8, TILE), jnp.int32),
            pltpu.SMEM((5, 8, TILE), jnp.int32),
            pltpu.VMEM((width, width), BF16),
            pltpu.VMEM((nodes, width), BF16),
            pltpu.VMEM((nodes, width), BF16),
            pltpu.VMEM((GROUP, nodes, TILE), BF16),
            pltpu.VMEM((GROUP, nodes, TILE), BF16),
            pltpu.VMEM((nodes, width), BF16),
            pltpu.VMEM((GROUP - 1, rows, TILE, TILE), BF16),
            pltpu.VMEM((panel_blocks, TILE, TILE), BF16),
            pltpu.VMEM((GROUP, quarter, width), F32),
            pltpu.VMEM((panel_blocks * SLOTS + 1, TILE, TILE), F32),
            pltpu.VMEM((2,) + chunk, BF16),
        ]
        + [pltpu.VMEM(chunk, BF16)] * 8
        + [
            pltpu.VMEM((nodes, width), BF16),
            pltpu.VMEM((GROUP, quarter, width), F32),
            pltpu.VMEM((quarter, width), F32),
            pltpu.VMEM((lines, part, width), F32),
            pltpu.VMEM((part, width), F32),
            pltpu.VMEM((run, tall, TILE), F32),
            pltpu.VMEM((part, width), F32),
            pltpu.VMEM((lines, part, width), BF16),
            pltpu.VMEM((GROUP, lines, part, width), BF16),
            pltpu.VMEM((width, width), F32),
        ]
        + pair * 5
        + [dma((3, rows)), dma((GROUP, rows))]
        + pair * 3
        + pair * 5
        + pair
        + [dma((lines,)), dma((lines,))]
        + [dma((run,)), dma((run,))] * 2
        + [dma((lines,)), dma((lines,))]
        + pair
        + [dma((8,))],
        compiler_params=pltpu.CompilerParams(
            collective_id=0, has_side_effects=True, vmem_limit_bytes=62 << 20
        ),
        name="layer",
    )(feats.reshape(rows, TILE, width), weight, vals, table, cot)
    return out, wgrad, grad


def solution(mesh, run=RUN):
    both = ("blk", "repl")
    in_specs = (
        P(both, None),
        P(),
        P(both, None, None, None),
        P(both, None),
        P(both),
        P(both, None),
    )
    out_specs = (P(both, None), P(), P(both, None))
    body = functools.partial(local, mesh.shape["blk"], run)
    return jax.shard_map(body, mesh=mesh, in_specs=in_specs, out_specs=out_specs, check_vma=False)
```

```python
import functools
import math

import jax
import jax.numpy as jnp
from jax import lax
from jax.experimental import pallas as pl
from jax.experimental.pallas import tpu as pltpu
from jax.sharding import PartitionSpec as P

TILE = 128
SLOTS = 8
REACH = 2
SPAN = 2 * REACH + 1
GROUP = 4
MESH = pl.DeviceIdType.MESH
BF16 = jnp.bfloat16
F32 = jnp.float32
RUN = 8
PLAN = "XZoooooooorrrzrrrrrffxffyffffc"


def place(nb, run):
    b = lax.axis_index("blk")
    r = lax.axis_index("repl")
    flip = 2 * ((b // run) % 2)
    g = (r + flip) % GROUP
    up = (b + 1) % nb
    down = (b + nb - 1) % nb
    r_up = (g + 2 * ((up // run) % 2)) % GROUP
    r_down = (g + 2 * ((down // run) % 2)) % GROUP
    p1 = r + 1 - 2 * (r % 2)
    p2 = (r + 2) % GROUP
    p3 = (p1 + 2) % GROUP
    return b, r, flip, g, up, down, r_up, r_down, p1, p2, p3


def partners(r):
    p1 = r + 1 - 2 * (r % 2)
    return r, p1, (r + 2) % GROUP, (p1 + 2) % GROUP


def remote(src, dst, send, recv, b, r):
    return pltpu.make_async_remote_copy(
        src_ref=src, dst_ref=dst, send_sem=send, recv_sem=recv, device_id=(b, r), device_id_type=MESH
    )


def greet(peers):
    barrier = pltpu.get_barrier_semaphore()
    for peer in peers:
        pl.semaphore_signal(barrier, inc=1, device_id=peer, device_id_type=MESH)
    pl.semaphore_wait(barrier, len(peers))


def ordered(member):
    own, core, chip, both = partners(member)
    return chip, both, core, own


def columns(ref, block):
    return ref.at[:, :, pl.ds(pl.multiple_of(block * TILE, TILE), TILE)]


def sorted_entries(dest):
    rows = lax.broadcasted_iota(jnp.int32, (TILE, TILE), 0)
    lanes = lax.broadcasted_iota(jnp.int32, (TILE, TILE), 1)
    across = jnp.broadcast_to(dest, (TILE, TILE))

    def count(mask, axis, value=1):
        return jnp.sum(jnp.where(mask, value, 0), axis=axis, keepdims=True)

    down = jnp.broadcast_to(count(rows == lanes, 1, across), (TILE, TILE))
    tie = (across == down) & (lanes < rows)
    rank = jnp.broadcast_to(count((across < down) | tie, 1), (TILE, TILE))
    repeat = jnp.broadcast_to(count(tie, 1), (TILE, TILE)) > 0
    hit = rank == lanes
    order = count(hit, 0, rows)
    before = jnp.where(count(hit & repeat, 0) > 0, lanes[0:1, :] - 1, TILE)
    owner = count(hit, 0, rows // SLOTS)
    upto = count(down <= lanes, 0)
    last = jnp.where(count(down == lanes, 0) > 0, upto - 1, TILE)
    return order, before, owner, last


def layer_kernel(
    nb, run, scale,
    feats, weight, vals, table, cot,
    out, grad, wgrad,
    win, vbuf, tbuf, smv, tsm, wv, cv, aggs, aggr, slope, bts, btp, wt, runs,
    far, su, sd, ru2, rd2, ru1, rd1, tot, rt, a0, s0, a1, s1, a2, s2, a3, b3, whole,
    fs, fr, us, ur, ds_, dr, us2, ur2, ds2, dr2, vs, vr, ts, tr, asend, arecv, bsend, brecv,
    vus, vur, vds, vdr, vus2, vur2, vds2, vdr2, gs, gr,
    w0s, w0r, w1s, w1r, w2s, w2r, w3s, w3r, x3s, x3r, x2s, x2r, x1s, x1r, x0s, x0r, loc,
):
    b, r, flip, g, up, down, r_up, r_down, p1, p2, p3 = place(nb, run)
    deep = nb // (2 * run)
    x_hi, y, z = (b // run) % 2, b // (2 * run), b % run
    core = r % 2
    xi = x_hi * 2 + r // 2
    wide = [(xi + i) % GROUP for i in range(1, GROUP)]
    tall = [(y + i) % deep for i in range(1, deep)]
    along = [(z + i) % run for i in range(1, run)]

    def at_x(i):
        return (y * 2 + i // 2) * run + z, (i % 2) * 2 + core

    def at_y(i):
        return (i * 2 + x_hi) * run + z, r

    def at_z(i):
        return (y * 2 + x_hi) * run + i, r

    panel_peers = (p1, p2, p3)
    order = (p2, p3, p1, r)
    greet(
        [(b, p) for p in panel_peers]
        + [(up, r_up), (down, r_down)]
        + [at_x(i) for i in wide]
        + [at_y(i) for i in tall]
        + [at_z(i) for i in along]
    )

    def group_of(member):
        return (member + flip) % GROUP

    sends = []

    def go(copy):
        copy.start()
        sends.append(copy)

    def landed(dst, recv):
        remote(dst, dst, fs.at[0], recv, b, p1).wait_recv()

    rows = vals.shape[0]
    panel_blocks = GROUP * rows
    dead = SPAN * panel_blocks

    def piece(panel, member):
        return win.at[pl.ds(panel * panel_blocks + member * rows, rows)]

    def tiles(member, c):
        return vbuf.at[pl.ds((member * rows + c) * SLOTS, SLOTS)]

    mine = columns(feats, g)
    for slot, p in enumerate((p2, p3, p1)):
        go(remote(columns(feats, group_of(p)), piece(2, r), fs.at[slot], fr.at[r], b, p))
    go(remote(mine, piece(1, r), us.at[0], ur.at[r], up, r_up))
    go(remote(mine, piece(3, r), ds_.at[0], dr.at[r], down, r_down))
    for slot, p in enumerate((p2, p3, p1)):
        go(remote(table, tbuf.at[r], ts.at[slot], tr.at[r], b, p))
    for c in range(rows):
        go(remote(vals.at[c], tiles(r, c), vs.at[0, c], vr.at[r, c], b, p2))
        go(remote(vals.at[c], tiles(r, c), vs.at[1, c], vr.at[r, c], b, p1))
    own = [
        pltpu.make_async_copy(table, tbuf.at[r], loc.at[0]),
        pltpu.make_async_copy(mine, piece(2, r), loc.at[1]),
        pltpu.make_async_copy(weight, wv, loc.at[2]),
        pltpu.make_async_copy(cot, cv, loc.at[3]),
    ] + [pltpu.make_async_copy(vals.at[c], tiles(r, c), loc.at[4 + c]) for c in range(rows)]
    for copy in own:
        copy.start()
    win[dead] = jnp.zeros((TILE, TILE), BF16)
    runs[TILE] = jnp.zeros((TILE, TILE), F32)

    for slot, p in ((1, p1), (2, p2), (3, p3)):
        landed(piece(2, p), fr.at[p])
        go(remote(piece(2, p), piece(1, p), us.at[slot], ur.at[p], up, r_up))
        go(remote(piece(2, p), piece(3, p), ds_.at[slot], dr.at[p], down, r_down))
    for p in panel_peers:
        landed(tbuf.at[p], tr.at[p])
    own[0].wait()
    dest = (tbuf[0] + tbuf[1]) + (tbuf[2] + tbuf[3])
    smv[0] = dest
    for line, value in enumerate(sorted_entries(dest[0:1, :])):
        smv[line + 1] = jnp.broadcast_to(value, (8, TILE))
    to_scalars = pltpu.make_async_copy(smv, tsm, loc.at[0])
    to_scalars.start()

    from_below = partners(r_down)
    from_above = partners(r_up)
    for slot in range(GROUP):
        i = from_below[slot]
        landed(piece(1, i), ur.at[i])
        go(remote(piece(1, i), piece(0, i), us2.at[slot], ur2.at[i], up, r_up))
        i = from_above[slot]
        landed(piece(3, i), dr.at[i])
        go(remote(piece(3, i), piece(4, i), ds2.at[slot], dr2.at[i], down, r_down))
        if slot < rows:
            landed(tiles(p2, slot), vr.at[p2, slot])
            go(remote(tiles(p2, slot), tiles(p2, slot), vs.at[2, slot], vr.at[p2, slot], b, p1))
    for i in range(GROUP):
        landed(piece(0, i), ur2.at[i])
        landed(piece(4, i), dr2.at[i])
    for copy in own[1:]:
        copy.wait()
    to_scalars.wait()
    for p in (p1, p3):
        for c in range(rows):
            landed(tiles(p, c), vr.at[p, c])

    half = rows // 2
    halves = [pl.ds(h * half * TILE, half * TILE) for h in range(2)]
    stay = []
    for h in range(2):
        for slot, q in enumerate(order):

            def one_row(kk, carry, q=q):
                first = (q * rows + kk) * SLOTS
                left = [vbuf[first + s] for s in range(SLOTS)]
                right = [win[tsm[0, 0, first + s]] for s in range(SLOTS)]
                total = jnp.dot(
                    jnp.concatenate(left, axis=1), jnp.concatenate(right, axis=0), preferred_element_type=F32
                )
                aggs[q, pl.ds(pl.multiple_of(kk * TILE, TILE), TILE), :] = total.astype(BF16)
                return carry

            lax.fori_loop(h * half, (h + 1) * half, one_row, 0)
            block, dst = aggs.at[q, halves[h]], aggr.at[g, halves[h]]
            if slot < 3:
                go(remote(block, dst, asend.at[slot, h], arecv.at[g, h], b, q))
            else:
                stay.append(pltpu.make_async_copy(block, dst, loc.at[4 + h]))
                stay[-1].start()

    def dense(t, carry):
        span = pl.ds(pl.multiple_of(t * TILE, TILE), TILE)
        agg = jnp.concatenate([aggr[i, span, :] for i in range(GROUP)], axis=1)
        pre = jnp.dot(agg, wv[...], preferred_element_type=F32)
        sigma = jax.nn.sigmoid(pre)
        out[span, :] = (pre * sigma).astype(BF16)
        slant = cv[span, :].astype(F32) * (sigma * (1.0 + pre * (1.0 - sigma)))
        slope[span, :] = slant.astype(BF16)
        return carry

    for h in range(2):
        stay[h].wait()
        for p in panel_peers:
            gp = group_of(p)
            landed(aggr.at[gp, halves[h]], arecv.at[gp, h])
        lax.fori_loop(h * half, (h + 1) * half, dense, 0)
        for slot, q in enumerate(order):
            part = wv[pl.ds(pl.multiple_of(group_of(q) * TILE, TILE), TILE), :]
            for t in range(h * half, (h + 1) * half):
                turned = lax.dot_general(
                    part, slope[pl.ds(t * TILE, TILE), :], (((1,), (1,)), ((), ())), preferred_element_type=F32
                )
                if slot < 3:
                    bts[slot, t] = turned.astype(BF16)
                else:
                    btp[r * rows + t] = turned.astype(BF16)
            if slot < 3:
                block, dst = bts.at[slot, pl.ds(h * half, half)], btp.at[pl.ds(r * rows + h * half, half)]
                go(remote(block, dst, bsend.at[slot, h], brecv.at[r, h], b, q))

    def weight_rows(i):
        wt[i] = lax.dot_general(aggr[i], slope[...], (((0,), (0,)), ((), ())), preferred_element_type=F32)

    for i in range(2):
        theirs = 2 * (1 - core) + i
        weight_rows(theirs)
        go(remote(wt.at[theirs], a0.at[i], w0s.at[i], w0r.at[i], b, p1))
    quarter = wt.shape[1]
    for i in range(2):
        weight_rows(2 * core + i)
    for i in range(2):
        landed(a0.at[i], w0r.at[i])
        s0[pl.ds(i * quarter, quarter), :] = wt[2 * core + i] + a0[i]
    block = 2 * quarter // deep
    for slot, i in enumerate(tall):
        part = s0.at[pl.ds(pl.multiple_of(i * block, block), block), :]
        go(remote(part, a1.at[y], w1s.at[slot], w1r.at[y], *at_y(i)))
    for p in panel_peers:
        for h in range(2):
            landed(btp.at[pl.ds(p * rows + h * half, half)], brecv.at[p, h])

    def eight(t, carry):
        first = t * 8
        terms = [
            jnp.dot(btp[tsm[3, 0, first + i]], vbuf[tsm[1, 0, first + i]], preferred_element_type=F32)
            for i in range(8)
        ]
        for i in range(8):
            runs[first + i] = terms[i] + runs[tsm[2, 0, first + i]]
        return carry

    lax.fori_loop(0, panel_blocks * SLOTS // 8, eight, 0)

    def share(panel, q, t):
        return runs[tsm[4, 0, panel * panel_blocks + q * rows + t]]

    order_below = ordered(r_down)
    order_above = ordered(r_up)
    steps = 2 * GROUP

    def tiles_of(members, step):
        q, h = members[step // 2], step % 2
        return q, q * 2 + h, range(h * half, (h + 1) * half)

    def outward(step):
        q, i, span = tiles_of(order, step)
        for j, t in enumerate(span):
            far[0, i, j] = share(4, q, t).astype(BF16)
            far[1, i, j] = share(0, q, t).astype(BF16)
        go(remote(far.at[0, i], ru2.at[i], vus.at[step], vur.at[i], up, r_up))
        go(remote(far.at[1, i], rd2.at[i], vds.at[step], vdr.at[i], down, r_down))

    def relay(step):
        q, i, span = tiles_of(order_below, step)
        landed(ru2.at[i], vur.at[i])
        for j, t in enumerate(span):
            su[i, j] = (ru2[i, j].astype(F32) + share(3, q, t)).astype(BF16)
        go(remote(su.at[i], ru1.at[i], vus2.at[step], vur2.at[i], up, r_up))
        q, i, span = tiles_of(order_above, step)
        landed(rd2.at[i], vdr.at[i])
        for j, t in enumerate(span):
            sd[i, j] = (rd2[i, j].astype(F32) + share(1, q, t)).astype(BF16)
        go(remote(sd.at[i], rd1.at[i], vds2.at[step], vdr2.at[i], down, r_down))

    def finish(step):
        q, i, span = tiles_of(order, step)
        h = step % 2
        landed(ru1.at[i], vur2.at[i])
        landed(rd1.at[i], vdr2.at[i])
        for j, t in enumerate(span):
            total = share(2, q, t) + (ru1[i, j].astype(F32) + rd1[i, j].astype(F32))
            if step < steps - 2:
                tot[i, j] = total.astype(BF16)
            else:
                rt[g * 2 + h, j] = total.astype(BF16)
        if step < steps - 2:
            go(remote(tot.at[i], rt.at[g * 2 + h], gs.at[step], gr.at[g * 2 + h], b, q))

    line = block // GROUP
    lanes = min(run, 4)
    high, broad = line // (run // lanes), wt.shape[2] // lanes

    def corner(ref, i):
        return ref.at[
            pl.ds(pl.multiple_of((i // lanes) * high, high), high),
            pl.ds(pl.multiple_of((i % lanes) * broad, broad), broad),
        ]

    def over_x():
        total = s0[pl.ds(pl.multiple_of(y * block, block), block), :]
        for i in tall:
            landed(a1.at[i], w1r.at[i])
            total = total + a1[i]
        s1[...] = total
        for slot, i in enumerate(wide):
            part = s1.at[pl.ds(pl.multiple_of(i * line, line), line), :]
            go(remote(part, a2.at[xi], w2s.at[slot], w2r.at[xi], *at_x(i)))

    def over_z():
        total = s1[pl.ds(pl.multiple_of(xi * line, line), line), :]
        for i in wide:
            landed(a2.at[i], w2r.at[i])
            total = total + a2[i]
        s2[...] = total
        for slot, i in enumerate(along):
            go(remote(corner(s2, i), a3.at[z], w3s.at[slot], w3r.at[z], *at_z(i)))

    def back_z():
        total = corner(s2, z)[...]
        for i in along:
            landed(a3.at[i], w3r.at[i])
            total = total + a3[i]
        corner(b3, z)[...] = total * scale
        for slot, i in enumerate(along):
            go(remote(corner(b3, z), corner(b3, z), x3s.at[slot], x3r.at[z], *at_z(i)))

    def back_x():
        for i in along:
            landed(corner(b3, i), x3r.at[i])
        whole[core, y, xi] = b3[...].astype(BF16)
        mine = whole.at[core, y, xi]
        for slot, i in enumerate(wide):
            go(remote(mine, mine, x2s.at[slot], x2r.at[xi], *at_x(i)))

    def hand_over(i, slot):
        theirs = whole.at[core, i]
        go(remote(theirs, theirs, x0s.at[slot], x0r.at[i], b, p1))

    def back_y():
        for i in wide:
            landed(whole.at[core, y, i], x2r.at[i])
        mine = whole.at[core, y]
        for slot, i in enumerate(tall):
            go(remote(mine, mine, x1s.at[slot], x1r.at[y], *at_y(i)))
        hand_over(y, 0)

    def back_core():
        for slot, i in enumerate(tall):
            landed(whole.at[core, i], x1r.at[i])
            hand_over(i, slot + 1)

    turns = {"o": iter(range(steps)), "r": iter(range(steps)), "f": iter(range(steps))}
    acts = {"o": outward, "r": relay, "f": finish}
    once = {"X": over_x, "Z": over_z, "z": back_z, "x": back_x, "y": back_y, "c": back_core}
    for turn in PLAN:
        if turn in acts:
            acts[turn](next(turns[turn]))
        else:
            once[turn]()

    eye = (
        lax.broadcasted_iota(jnp.int32, (TILE, TILE), 0) == lax.broadcasted_iota(jnp.int32, (TILE, TILE), 1)
    ).astype(BF16)
    for p in panel_peers:
        gp = group_of(p)
        for h in range(2):
            landed(rt.at[gp * 2 + h], gr.at[gp * 2 + h])
    for i in range(GROUP):
        for t in range(rows):
            turned = lax.dot_general(eye, rt[i * 2 + t // half, t % half], (((1,), (1,)), ((), ())), preferred_element_type=F32)
            grad[pl.ds(t * TILE, TILE), pl.ds(i * TILE, TILE)] = turned.astype(BF16)
    for i in range(deep):
        landed(whole.at[1 - core, i], x0r.at[i])
    for c in range(2):
        for i in range(deep):
            for j in range(GROUP):
                wgrad[pl.ds((c * deep + i) * block + j * line, line), :] = whole[c, i, j].astype(F32)
    for copy in sends:
        copy.wait_send()


def window_table(tile_cols, tile_count, panel_blocks, nb):
    center = lax.axis_index("blk")
    offset = (tile_cols // panel_blocks - center) % nb
    offset = jnp.where(offset > REACH, offset - nb, offset)
    index = (offset + REACH) * panel_blocks + tile_cols % panel_blocks
    dead = SPAN * panel_blocks
    alive = jnp.arange(SLOTS, dtype=jnp.int32)[None, :] < tile_count[:, None]
    index = jnp.where(alive, jnp.clip(index, 0, dead - 1), dead).astype(jnp.int32)
    line = jnp.tile(index.reshape(1, -1), (8, GROUP))
    lane = lax.broadcasted_iota(jnp.int32, line.shape, 1)
    return jnp.where(lane // index.size == lax.axis_index("repl"), line, 0)


def local(nb, run, feats, weight, vals, cols, count, cot):
    nodes, width = feats.shape
    rows = nodes // TILE
    panel_blocks = GROUP * rows
    deep = nb // (2 * run)
    table = window_table(cols, count, panel_blocks, nb)
    anywhere = pl.BlockSpec(memory_space=pl.ANY)
    dma = pltpu.SemaphoreType.DMA
    shape = jax.ShapeDtypeStruct
    chunk = (2 * GROUP, rows // 2, TILE, TILE)
    quarter = width // GROUP
    block = 2 * quarter // deep
    line = block // GROUP
    lanes = min(run, 4)
    corner = (line // (run // lanes), width // lanes)
    in_hbm = pl.BlockSpec(memory_space=pltpu.HBM)
    in_vmem = pl.BlockSpec(memory_space=pltpu.VMEM)
    pair = [dma((GROUP,)), dma((GROUP,))]
    out, grad, wgrad = pl.pallas_call(
        functools.partial(layer_kernel, nb, run, 1.0 / math.sqrt(nodes * GROUP * nb)),
        out_shape=(
            shape((nodes, width), BF16),
            shape((nodes, width), BF16),
            shape((width, width), F32),
        ),
        in_specs=[in_hbm, in_hbm, in_hbm, anywhere, in_hbm],
        out_specs=(in_vmem,) * 3,
        scratch_shapes=[
            pltpu.VMEM((SPAN * panel_blocks + 1, TILE, TILE), BF16),
            pltpu.VMEM((panel_blocks * SLOTS, TILE, TILE), BF16),
            pltpu.VMEM((GROUP, 8, TILE), jnp.int32),
            pltpu.VMEM((5, 8, TILE), jnp.int32),
            pltpu.SMEM((5, 8, TILE), jnp.int32),
            pltpu.VMEM((width, width), BF16),
            pltpu.VMEM((nodes, width), BF16),
            pltpu.VMEM((GROUP, nodes, TILE), BF16),
            pltpu.VMEM((GROUP, nodes, TILE), BF16),
            pltpu.VMEM((nodes, width), BF16),
            pltpu.VMEM((GROUP - 1, rows, TILE, TILE), BF16),
            pltpu.VMEM((panel_blocks, TILE, TILE), BF16),
            pltpu.VMEM((GROUP, quarter, width), F32),
            pltpu.VMEM((panel_blocks * SLOTS + 1, TILE, TILE), F32),
            pltpu.VMEM((2,) + chunk, BF16),
        ]
        + [pltpu.VMEM(chunk, BF16)] * 8
        + [
            pltpu.VMEM((2, quarter, width), F32),
            pltpu.VMEM((2 * quarter, width), F32),
            pltpu.VMEM((deep, block, width), F32),
            pltpu.VMEM((block, width), F32),
            pltpu.VMEM((GROUP, line, width), F32),
            pltpu.VMEM((line, width), F32),
            pltpu.VMEM((run,) + corner, F32),
            pltpu.VMEM((line, width), F32),
            pltpu.VMEM((2, deep, GROUP, line, width), BF16),
        ]
        + pair * 5
        + [dma((3, rows)), dma((GROUP, rows))]
        + pair
        + [dma((3, 2)), dma((GROUP, 2))] * 2
        + [dma((2 * GROUP,)), dma((2 * GROUP,))] * 5
        + [dma((2,)), dma((2,))]
        + [dma((deep,)), dma((deep,))]
        + pair
        + [dma((run,)), dma((run,))] * 2
        + pair
        + [dma((deep,)), dma((deep,))] * 2
        + [dma((8,))],
        compiler_params=pltpu.CompilerParams(
            collective_id=0, has_side_effects=True, vmem_limit_bytes=50 << 20
        ),
        name="layer",
    )(feats.reshape(rows, TILE, width), weight, vals, table, cot)
    return out, wgrad, grad


def solution(mesh, run=RUN):
    both = ("blk", "repl")
    in_specs = (
        P(both, None),
        P(),
        P(both, None, None, None),
        P(both, None),
        P(both),
        P(both, None),
    )
    out_specs = (P(both, None), P(), P(both, None))
    body = functools.partial(local, mesh.shape["blk"], run)
    return jax.shard_map(body, mesh=mesh, in_specs=in_specs, out_specs=out_specs, check_vma=False)
```

```python
import functools
import math

import jax
import jax.numpy as jnp
from jax import lax
from jax.experimental import pallas as pl
from jax.experimental.pallas import tpu as pltpu
from jax.sharding import PartitionSpec as P

TILE = 128
SLOTS = 8
REACH = 2
SPAN = 2 * REACH + 1
GROUP = 4
MESH = pl.DeviceIdType.MESH
BF16 = jnp.bfloat16
F32 = jnp.float32
RUN = 8
PLAN = "XZoooooooorrrzrrrrrxyffcffffff"


def place(nb, run):
    b = lax.axis_index("blk")
    r = lax.axis_index("repl")
    flip = 2 * ((b // run) % 2)
    g = (r + flip) % GROUP
    up = (b + 1) % nb
    down = (b + nb - 1) % nb
    r_up = (g + 2 * ((up // run) % 2)) % GROUP
    r_down = (g + 2 * ((down // run) % 2)) % GROUP
    p1 = r + 1 - 2 * (r % 2)
    p2 = (r + 2) % GROUP
    p3 = (p1 + 2) % GROUP
    return b, r, flip, g, up, down, r_up, r_down, p1, p2, p3


def partners(r):
    p1 = r + 1 - 2 * (r % 2)
    return r, p1, (r + 2) % GROUP, (p1 + 2) % GROUP


def remote(src, dst, send, recv, b, r):
    return pltpu.make_async_remote_copy(
        src_ref=src, dst_ref=dst, send_sem=send, recv_sem=recv, device_id=(b, r), device_id_type=MESH
    )


def greet(peers):
    barrier = pltpu.get_barrier_semaphore()
    for peer in peers:
        pl.semaphore_signal(barrier, inc=1, device_id=peer, device_id_type=MESH)
    pl.semaphore_wait(barrier, len(peers))


def ordered(member):
    own, core, chip, both = partners(member)
    return chip, both, core, own


def columns(ref, block):
    return ref.at[:, :, pl.ds(pl.multiple_of(block * TILE, TILE), TILE)]


def sorted_entries(dest):
    rows = lax.broadcasted_iota(jnp.int32, (TILE, TILE), 0)
    lanes = lax.broadcasted_iota(jnp.int32, (TILE, TILE), 1)
    across = jnp.broadcast_to(dest, (TILE, TILE))

    def count(mask, axis, value=1):
        return jnp.sum(jnp.where(mask, value, 0), axis=axis, keepdims=True)

    down = jnp.broadcast_to(count(rows == lanes, 1, across), (TILE, TILE))
    tie = (across == down) & (lanes < rows)
    rank = jnp.broadcast_to(count((across < down) | tie, 1), (TILE, TILE))
    repeat = jnp.broadcast_to(count(tie, 1), (TILE, TILE)) > 0
    hit = rank == lanes
    order = count(hit, 0, rows)
    before = jnp.where(count(hit & repeat, 0) > 0, lanes[0:1, :] - 1, TILE)
    owner = count(hit, 0, rows // SLOTS)
    upto = count(down <= lanes, 0)
    last = jnp.where(count(down == lanes, 0) > 0, upto - 1, TILE)
    return order, before, owner, last


def layer_kernel(
    nb, run, scale,
    feats, weight, vals, table, cot,
    out, grad, wgrad,
    win, vbuf, tbuf, smv, tsm, wv, cv, aggs, aggr, slope, bts, btp, wt, runs,
    far, su, sd, ru2, rd2, ru1, rd1, tot, rt, a0, s0, a1, s1, a2, s2, a3, b3, whole,
    fs, fr, us, ur, ds_, dr, us2, ur2, ds2, dr2, vs, vr, ts, tr, asend, arecv, bsend, brecv,
    vus, vur, vds, vdr, vus2, vur2, vds2, vdr2, gs, gr,
    w0s, w0r, w1s, w1r, w2s, w2r, w3s, w3r, x3s, x3r, x2s, x2r, x1s, x1r, x0s, x0r, loc,
):
    b, r, flip, g, up, down, r_up, r_down, p1, p2, p3 = place(nb, run)
    deep = nb // (2 * run)
    x_hi, y, z = (b // run) % 2, b // (2 * run), b % run
    core = r % 2
    xi = x_hi * 2 + r // 2
    wide = [(xi + i) % GROUP for i in range(1, GROUP)]
    tall = [(y + i) % deep for i in range(1, deep)]
    along = [(z + i) % run for i in range(1, run)]

    def at_x(i):
        return (y * 2 + i // 2) * run + z, (i % 2) * 2 + core

    def at_y(i):
        return (i * 2 + x_hi) * run + z, r

    def at_z(i):
        return (y * 2 + x_hi) * run + i, r

    panel_peers = (p1, p2, p3)
    order = (p2, p3, p1, r)
    greet(
        [(b, p) for p in panel_peers]
        + [(up, r_up), (down, r_down)]
        + [at_x(i) for i in wide]
        + [at_y(i) for i in tall]
        + [at_z(i) for i in along]
    )

    def group_of(member):
        return (member + flip) % GROUP

    sends = []

    def go(copy):
        copy.start()
        sends.append(copy)

    def landed(dst, recv):
        remote(dst, dst, fs.at[0], recv, b, p1).wait_recv()

    rows = vals.shape[0]
    panel_blocks = GROUP * rows
    dead = SPAN * panel_blocks

    def piece(panel, member):
        return win.at[pl.ds(panel * panel_blocks + member * rows, rows)]

    def tiles(member, c):
        return vbuf.at[pl.ds((member * rows + c) * SLOTS, SLOTS)]

    mine = columns(feats, g)
    for slot, p in enumerate((p2, p3, p1)):
        go(remote(columns(feats, group_of(p)), piece(2, r), fs.at[slot], fr.at[r], b, p))
    go(remote(mine, piece(1, r), us.at[0], ur.at[r], up, r_up))
    go(remote(mine, piece(3, r), ds_.at[0], dr.at[r], down, r_down))
    for slot, p in enumerate((p2, p3, p1)):
        go(remote(table, tbuf.at[r], ts.at[slot], tr.at[r], b, p))
    for c in range(rows):
        go(remote(vals.at[c], tiles(r, c), vs.at[0, c], vr.at[r, c], b, p2))
        go(remote(vals.at[c], tiles(r, c), vs.at[1, c], vr.at[r, c], b, p1))
    own = [
        pltpu.make_async_copy(table, tbuf.at[r], loc.at[0]),
        pltpu.make_async_copy(mine, piece(2, r), loc.at[1]),
        pltpu.make_async_copy(weight, wv, loc.at[2]),
        pltpu.make_async_copy(cot, cv, loc.at[3]),
    ] + [pltpu.make_async_copy(vals.at[c], tiles(r, c), loc.at[4 + c]) for c in range(rows)]
    for copy in own:
        copy.start()
    win[dead] = jnp.zeros((TILE, TILE), BF16)
    runs[TILE] = jnp.zeros((TILE, TILE), F32)

    for slot, p in ((1, p1), (2, p2), (3, p3)):
        landed(piece(2, p), fr.at[p])
        go(remote(piece(2, p), piece(1, p), us.at[slot], ur.at[p], up, r_up))
        go(remote(piece(2, p), piece(3, p), ds_.at[slot], dr.at[p], down, r_down))
    for p in panel_peers:
        landed(tbuf.at[p], tr.at[p])
    own[0].wait()
    dest = (tbuf[0] + tbuf[1]) + (tbuf[2] + tbuf[3])
    smv[0] = dest
    for line, value in enumerate(sorted_entries(dest[0:1, :])):
        smv[line + 1] = jnp.broadcast_to(value, (8, TILE))
    to_scalars = pltpu.make_async_copy(smv, tsm, loc.at[0])
    to_scalars.start()

    from_below = partners(r_down)
    from_above = partners(r_up)
    for slot in range(GROUP):
        i = from_below[slot]
        landed(piece(1, i), ur.at[i])
        go(remote(piece(1, i), piece(0, i), us2.at[slot], ur2.at[i], up, r_up))
        i = from_above[slot]
        landed(piece(3, i), dr.at[i])
        go(remote(piece(3, i), piece(4, i), ds2.at[slot], dr2.at[i], down, r_down))

    def tiles_on(c):
        landed(tiles(p2, c), vr.at[p2, c])
        go(remote(tiles(p2, c), tiles(p2, c), vs.at[2, c], vr.at[p2, c], b, p1))

    half = rows // 2
    for c in range(half):
        tiles_on(c)
    for i in range(GROUP):
        landed(piece(0, i), ur2.at[i])
        landed(piece(4, i), dr2.at[i])
    for copy in own[1:]:
        copy.wait()
    to_scalars.wait()

    halves = [pl.ds(h * half * TILE, half * TILE) for h in range(2)]
    stay = []
    for h in range(2):
        for c in range(h * half, (h + 1) * half):
            if h == 1:
                tiles_on(c)
            landed(tiles(p1, c), vr.at[p1, c])
        for c in range(h * half, (h + 1) * half):
            landed(tiles(p3, c), vr.at[p3, c])
        for slot, q in enumerate(order):

            def one_row(kk, carry, q=q):
                first = (q * rows + kk) * SLOTS
                left = [vbuf[first + s] for s in range(SLOTS)]
                right = [win[tsm[0, 0, first + s]] for s in range(SLOTS)]
                total = jnp.dot(
                    jnp.concatenate(left, axis=1), jnp.concatenate(right, axis=0), preferred_element_type=F32
                )
                aggs[q, pl.ds(pl.multiple_of(kk * TILE, TILE), TILE), :] = total.astype(BF16)
                return carry

            lax.fori_loop(h * half, (h + 1) * half, one_row, 0)
            block, dst = aggs.at[q, halves[h]], aggr.at[g, halves[h]]
            if slot < 3:
                go(remote(block, dst, asend.at[slot, h], arecv.at[g, h], b, q))
            else:
                stay.append(pltpu.make_async_copy(block, dst, loc.at[4 + h]))
                stay[-1].start()

    def dense(t, carry):
        span = pl.ds(pl.multiple_of(t * TILE, TILE), TILE)
        agg = jnp.concatenate([aggr[i, span, :] for i in range(GROUP)], axis=1)
        pre = jnp.dot(agg, wv[...], preferred_element_type=F32)
        sigma = jax.nn.sigmoid(pre)
        out[span, :] = (pre * sigma).astype(BF16)
        slant = cv[span, :].astype(F32) * (sigma * (1.0 + pre * (1.0 - sigma)))
        slope[span, :] = slant.astype(BF16)
        return carry

    for h in range(2):
        stay[h].wait()
        for p in panel_peers:
            gp = group_of(p)
            landed(aggr.at[gp, halves[h]], arecv.at[gp, h])
        lax.fori_loop(h * half, (h + 1) * half, dense, 0)
        for slot, q in enumerate(order):
            part = wv[pl.ds(pl.multiple_of(group_of(q) * TILE, TILE), TILE), :]
            for t in range(h * half, (h + 1) * half):
                turned = lax.dot_general(
                    part, slope[pl.ds(t * TILE, TILE), :], (((1,), (1,)), ((), ())), preferred_element_type=F32
                )
                if slot < 3:
                    bts[slot, t] = turned.astype(BF16)
                else:
                    btp[r * rows + t] = turned.astype(BF16)
            if slot < 3:
                block, dst = bts.at[slot, pl.ds(h * half, half)], btp.at[pl.ds(r * rows + h * half, half)]
                go(remote(block, dst, bsend.at[slot, h], brecv.at[r, h], b, q))

    def weight_rows(i):
        wt[i] = lax.dot_general(aggr[i], slope[...], (((0,), (0,)), ((), ())), preferred_element_type=F32)

    for i in range(2):
        theirs = 2 * (1 - core) + i
        weight_rows(theirs)
        go(remote(wt.at[theirs], a0.at[i], w0s.at[i], w0r.at[i], b, p1))
    quarter = wt.shape[1]
    for i in range(2):
        weight_rows(2 * core + i)
    for i in range(2):
        landed(a0.at[i], w0r.at[i])
        s0[pl.ds(i * quarter, quarter), :] = wt[2 * core + i] + a0[i]
    block = 2 * quarter // deep
    for slot, i in enumerate(tall):
        part = s0.at[pl.ds(pl.multiple_of(i * block, block), block), :]
        go(remote(part, a1.at[y], w1s.at[slot], w1r.at[y], *at_y(i)))
    for p in panel_peers:
        for h in range(2):
            landed(btp.at[pl.ds(p * rows + h * half, half)], brecv.at[p, h])

    def eight(t, carry):
        first = t * 8
        terms = [
            jnp.dot(btp[tsm[3, 0, first + i]], vbuf[tsm[1, 0, first + i]], preferred_element_type=F32)
            for i in range(8)
        ]
        for i in range(8):
            runs[first + i] = terms[i] + runs[tsm[2, 0, first + i]]
        return carry

    lax.fori_loop(0, panel_blocks * SLOTS // 8, eight, 0)

    def share(panel, q, t):
        return runs[tsm[4, 0, panel * panel_blocks + q * rows + t]]

    order_below = ordered(r_down)
    order_above = ordered(r_up)
    steps = 2 * GROUP

    def tiles_of(members, step):
        q, h = members[step // 2], step % 2
        return q, q * 2 + h, range(h * half, (h + 1) * half)

    def outward(step):
        q, i, span = tiles_of(order, step)
        for j, t in enumerate(span):
            far[0, i, j] = share(4, q, t).astype(BF16)
            far[1, i, j] = share(0, q, t).astype(BF16)
        go(remote(far.at[0, i], ru2.at[i], vus.at[step], vur.at[i], up, r_up))
        go(remote(far.at[1, i], rd2.at[i], vds.at[step], vdr.at[i], down, r_down))

    def relay(step):
        q, i, span = tiles_of(order_below, step)
        landed(ru2.at[i], vur.at[i])
        for j, t in enumerate(span):
            su[i, j] = (ru2[i, j].astype(F32) + share(3, q, t)).astype(BF16)
        go(remote(su.at[i], ru1.at[i], vus2.at[step], vur2.at[i], up, r_up))
        q, i, span = tiles_of(order_above, step)
        landed(rd2.at[i], vdr.at[i])
        for j, t in enumerate(span):
            sd[i, j] = (rd2[i, j].astype(F32) + share(1, q, t)).astype(BF16)
        go(remote(sd.at[i], rd1.at[i], vds2.at[step], vdr2.at[i], down, r_down))

    def finish(step):
        q, i, span = tiles_of(order, step)
        h = step % 2
        landed(ru1.at[i], vur2.at[i])
        landed(rd1.at[i], vdr2.at[i])
        for j, t in enumerate(span):
            total = share(2, q, t) + (ru1[i, j].astype(F32) + rd1[i, j].astype(F32))
            if step < steps - 2:
                tot[i, j] = total.astype(BF16)
            else:
                rt[g * 2 + h, j] = total.astype(BF16)
        if step < steps - 2:
            go(remote(tot.at[i], rt.at[g * 2 + h], gs.at[step], gr.at[g * 2 + h], b, q))

    line = block // GROUP
    lanes = min(run, 4)
    high, broad = line // (run // lanes), wt.shape[2] // lanes

    def corner(ref, i):
        return ref.at[
            pl.ds(pl.multiple_of((i // lanes) * high, high), high),
            pl.ds(pl.multiple_of((i % lanes) * broad, broad), broad),
        ]

    def over_x():
        total = s0[pl.ds(pl.multiple_of(y * block, block), block), :]
        for i in tall:
            landed(a1.at[i], w1r.at[i])
            total = total + a1[i]
        s1[...] = total
        for slot, i in enumerate(wide):
            part = s1.at[pl.ds(pl.multiple_of(i * line, line), line), :]
            go(remote(part, a2.at[xi], w2s.at[slot], w2r.at[xi], *at_x(i)))

    def over_z():
        total = s1[pl.ds(pl.multiple_of(xi * line, line), line), :]
        for i in wide:
            landed(a2.at[i], w2r.at[i])
            total = total + a2[i]
        s2[...] = total
        for slot, i in enumerate(along):
            go(remote(corner(s2, i), a3.at[z], w3s.at[slot], w3r.at[z], *at_z(i)))

    def back_z():
        total = corner(s2, z)[...]
        for i in along:
            landed(a3.at[i], w3r.at[i])
            total = total + a3[i]
        corner(b3, z)[...] = total * scale
        for slot, i in enumerate(along):
            go(remote(corner(b3, z), corner(b3, z), x3s.at[slot], x3r.at[z], *at_z(i)))

    def back_x():
        for i in along:
            landed(corner(b3, i), x3r.at[i])
        whole[core, y, xi] = b3[...].astype(BF16)
        mine = whole.at[core, y, xi]
        for slot, i in enumerate(wide):
            go(remote(mine, mine, x2s.at[slot], x2r.at[xi], *at_x(i)))

    def hand_over(i, slot):
        theirs = whole.at[core, i]
        go(remote(theirs, theirs, x0s.at[slot], x0r.at[i], b, p1))

    def back_y():
        for i in wide:
            landed(whole.at[core, y, i], x2r.at[i])
        mine = whole.at[core, y]
        for slot, i in enumerate(tall):
            go(remote(mine, mine, x1s.at[slot], x1r.at[y], *at_y(i)))
        hand_over(y, 0)

    def back_core():
        for slot, i in enumerate(tall):
            landed(whole.at[core, i], x1r.at[i])
            hand_over(i, slot + 1)

    turns = {"o": iter(range(steps)), "r": iter(range(steps)), "f": iter(range(steps))}
    acts = {"o": outward, "r": relay, "f": finish}
    once = {"X": over_x, "Z": over_z, "z": back_z, "x": back_x, "y": back_y, "c": back_core}
    for turn in PLAN:
        if turn in acts:
            acts[turn](next(turns[turn]))
        else:
            once[turn]()

    eye = (
        lax.broadcasted_iota(jnp.int32, (TILE, TILE), 0) == lax.broadcasted_iota(jnp.int32, (TILE, TILE), 1)
    ).astype(BF16)
    for p in panel_peers:
        gp = group_of(p)
        for h in range(2):
            landed(rt.at[gp * 2 + h], gr.at[gp * 2 + h])
    for i in range(GROUP):
        for t in range(rows):
            turned = lax.dot_general(eye, rt[i * 2 + t // half, t % half], (((1,), (1,)), ((), ())), preferred_element_type=F32)
            grad[pl.ds(t * TILE, TILE), pl.ds(i * TILE, TILE)] = turned.astype(BF16)
    for i in range(deep):
        landed(whole.at[1 - core, i], x0r.at[i])
    for c in range(2):
        for i in range(deep):
            for j in range(GROUP):
                wgrad[pl.ds((c * deep + i) * block + j * line, line), :] = whole[c, i, j].astype(F32)
    for copy in sends:
        copy.wait_send()


def window_table(tile_cols, tile_count, panel_blocks, nb):
    center = lax.axis_index("blk")
    offset = (tile_cols // panel_blocks - center) % nb
    offset = jnp.where(offset > REACH, offset - nb, offset)
    index = (offset + REACH) * panel_blocks + tile_cols % panel_blocks
    dead = SPAN * panel_blocks
    alive = jnp.arange(SLOTS, dtype=jnp.int32)[None, :] < tile_count[:, None]
    index = jnp.where(alive, jnp.clip(index, 0, dead - 1), dead).astype(jnp.int32)
    line = jnp.tile(index.reshape(1, -1), (8, GROUP))
    lane = lax.broadcasted_iota(jnp.int32, line.shape, 1)
    return jnp.where(lane // index.size == lax.axis_index("repl"), line, 0)


def local(nb, run, feats, weight, vals, cols, count, cot):
    nodes, width = feats.shape
    rows = nodes // TILE
    panel_blocks = GROUP * rows
    deep = nb // (2 * run)
    table = window_table(cols, count, panel_blocks, nb)
    anywhere = pl.BlockSpec(memory_space=pl.ANY)
    dma = pltpu.SemaphoreType.DMA
    shape = jax.ShapeDtypeStruct
    chunk = (2 * GROUP, rows // 2, TILE, TILE)
    quarter = width // GROUP
    block = 2 * quarter // deep
    line = block // GROUP
    lanes = min(run, 4)
    corner = (line // (run // lanes), width // lanes)
    in_hbm = pl.BlockSpec(memory_space=pltpu.HBM)
    in_vmem = pl.BlockSpec(memory_space=pltpu.VMEM)
    pair = [dma((GROUP,)), dma((GROUP,))]
    out, grad, wgrad = pl.pallas_call(
        functools.partial(layer_kernel, nb, run, 1.0 / math.sqrt(nodes * GROUP * nb)),
        out_shape=(
            shape((nodes, width), BF16),
            shape((nodes, width), BF16),
            shape((width, width), F32),
        ),
        in_specs=[in_hbm, in_hbm, in_hbm, anywhere, in_hbm],
        out_specs=(in_vmem,) * 3,
        scratch_shapes=[
            pltpu.VMEM((SPAN * panel_blocks + 1, TILE, TILE), BF16),
            pltpu.VMEM((panel_blocks * SLOTS, TILE, TILE), BF16),
            pltpu.VMEM((GROUP, 8, TILE), jnp.int32),
            pltpu.VMEM((5, 8, TILE), jnp.int32),
            pltpu.SMEM((5, 8, TILE), jnp.int32),
            pltpu.VMEM((width, width), BF16),
            pltpu.VMEM((nodes, width), BF16),
            pltpu.VMEM((GROUP, nodes, TILE), BF16),
            pltpu.VMEM((GROUP, nodes, TILE), BF16),
            pltpu.VMEM((nodes, width), BF16),
            pltpu.VMEM((GROUP - 1, rows, TILE, TILE), BF16),
            pltpu.VMEM((panel_blocks, TILE, TILE), BF16),
            pltpu.VMEM((GROUP, quarter, width), F32),
            pltpu.VMEM((panel_blocks * SLOTS + 1, TILE, TILE), F32),
            pltpu.VMEM((2,) + chunk, BF16),
        ]
        + [pltpu.VMEM(chunk, BF16)] * 8
        + [
            pltpu.VMEM((2, quarter, width), F32),
            pltpu.VMEM((2 * quarter, width), F32),
            pltpu.VMEM((deep, block, width), F32),
            pltpu.VMEM((block, width), F32),
            pltpu.VMEM((GROUP, line, width), F32),
            pltpu.VMEM((line, width), F32),
            pltpu.VMEM((run,) + corner, F32),
            pltpu.VMEM((line, width), F32),
            pltpu.VMEM((2, deep, GROUP, line, width), BF16),
        ]
        + pair * 5
        + [dma((3, rows)), dma((GROUP, rows))]
        + pair
        + [dma((3, 2)), dma((GROUP, 2))] * 2
        + [dma((2 * GROUP,)), dma((2 * GROUP,))] * 5
        + [dma((2,)), dma((2,))]
        + [dma((deep,)), dma((deep,))]
        + pair
        + [dma((run,)), dma((run,))] * 2
        + pair
        + [dma((deep,)), dma((deep,))] * 2
        + [dma((8,))],
        compiler_params=pltpu.CompilerParams(
            collective_id=0, has_side_effects=True, vmem_limit_bytes=50 << 20
        ),
        name="layer",
    )(
        *(pltpu.with_memory_space_constraint(x, pltpu.HBM) for x in (feats.reshape(rows, TILE, width), weight, vals)),
        table,
        pltpu.with_memory_space_constraint(cot, pltpu.HBM),
    )
    return out, wgrad, grad


def solution(mesh, run=RUN):
    both = ("blk", "repl")
    in_specs = (
        P(both, None),
        P(),
        P(both, None, None, None),
        P(both, None),
        P(both),
        P(both, None),
    )
    out_specs = (P(both, None), P(), P(both, None))
    body = functools.partial(local, mesh.shape["blk"], run)
    return jax.shard_map(body, mesh=mesh, in_specs=in_specs, out_specs=out_specs, check_vma=False)
```

```python
import functools
import math

import jax
import jax.numpy as jnp
from jax import lax
from jax.experimental import pallas as pl
from jax.experimental.pallas import tpu as pltpu
from jax.sharding import PartitionSpec as P

TILE = 128
SLOTS = 8
REACH = 2
SPAN = 2 * REACH + 1
GROUP = 4
MESH = pl.DeviceIdType.MESH
BF16 = jnp.bfloat16
F32 = jnp.float32
RUN = 8
PLAN = "ooooooooXrZrrrrzrrrxfyfcffffff"


def place(nb, run):
    b = lax.axis_index("blk")
    r = lax.axis_index("repl")
    flip = 2 * ((b // run) % 2)
    g = (r + flip) % GROUP
    up = (b + 1) % nb
    down = (b + nb - 1) % nb
    r_up = (g + 2 * ((up // run) % 2)) % GROUP
    r_down = (g + 2 * ((down // run) % 2)) % GROUP
    p1 = r + 1 - 2 * (r % 2)
    p2 = (r + 2) % GROUP
    p3 = (p1 + 2) % GROUP
    return b, r, flip, g, up, down, r_up, r_down, p1, p2, p3


def partners(r):
    p1 = r + 1 - 2 * (r % 2)
    return r, p1, (r + 2) % GROUP, (p1 + 2) % GROUP


def remote(src, dst, send, recv, b, r):
    return pltpu.make_async_remote_copy(
        src_ref=src, dst_ref=dst, send_sem=send, recv_sem=recv, device_id=(b, r), device_id_type=MESH
    )


def greet(peers):
    barrier = pltpu.get_barrier_semaphore()
    for peer in peers:
        pl.semaphore_signal(barrier, inc=1, device_id=peer, device_id_type=MESH)
    pl.semaphore_wait(barrier, len(peers))


def ordered(member):
    own, core, chip, both = partners(member)
    return chip, both, core, own


def columns(ref, block):
    return ref.at[:, :, pl.ds(pl.multiple_of(block * TILE, TILE), TILE)]


def sorted_entries(dest):
    rows = lax.broadcasted_iota(jnp.int32, (TILE, TILE), 0)
    lanes = lax.broadcasted_iota(jnp.int32, (TILE, TILE), 1)
    across = jnp.broadcast_to(dest, (TILE, TILE))

    def count(mask, axis, value=1):
        return jnp.sum(jnp.where(mask, value, 0), axis=axis, keepdims=True)

    down = jnp.broadcast_to(count(rows == lanes, 1, across), (TILE, TILE))
    tie = (across == down) & (lanes < rows)
    rank = jnp.broadcast_to(count((across < down) | tie, 1), (TILE, TILE))
    repeat = jnp.broadcast_to(count(tie, 1), (TILE, TILE)) > 0
    hit = rank == lanes
    order = count(hit, 0, rows)
    before = jnp.where(count(hit & repeat, 0) > 0, lanes[0:1, :] - 1, TILE)
    owner = count(hit, 0, rows // SLOTS)
    upto = count(down <= lanes, 0)
    last = jnp.where(count(down == lanes, 0) > 0, upto - 1, TILE)
    return order, before, owner, last


def layer_kernel(
    nb, run, scale,
    feats, weight, vals, table, cot,
    out, grad, wgrad,
    win, vbuf, tbuf, smv, tsm, wv, cv, aggs, aggr, slope, bts, btp, wt, runs,
    far, su, sd, ru2, rd2, ru1, rd1, tot, rt, a0, s0, a1, s1, a2, s2, a3, b3, whole,
    fs, fr, us, ur, ds_, dr, us2, ur2, ds2, dr2, vs, vr, ts, tr, asend, arecv, bsend, brecv,
    vus, vur, vds, vdr, vus2, vur2, vds2, vdr2, gs, gr,
    w0s, w0r, w1s, w1r, w2s, w2r, w3s, w3r, x3s, x3r, x2s, x2r, x1s, x1r, x0s, x0r, loc,
):
    b, r, flip, g, up, down, r_up, r_down, p1, p2, p3 = place(nb, run)
    deep = nb // (2 * run)
    x_hi, y, z = (b // run) % 2, b // (2 * run), b % run
    core = r % 2
    xi = x_hi * 2 + r // 2
    wide = [(xi + i) % GROUP for i in range(1, GROUP)]
    tall = [(y + i) % deep for i in range(1, deep)]
    along = [(z + i) % run for i in range(1, run)]

    def at_x(i):
        return (y * 2 + i // 2) * run + z, (i % 2) * 2 + core

    def at_y(i):
        return (i * 2 + x_hi) * run + z, r

    def at_z(i):
        return (y * 2 + x_hi) * run + i, r

    panel_peers = (p1, p2, p3)
    order = (p2, p3, p1, r)
    greet(
        [(b, p) for p in panel_peers]
        + [(up, r_up), (down, r_down)]
        + [at_x(i) for i in wide]
        + [at_y(i) for i in tall]
        + [at_z(i) for i in along]
    )

    def group_of(member):
        return (member + flip) % GROUP

    sends = []

    def go(copy):
        copy.start()
        sends.append(copy)

    def landed(dst, recv):
        remote(dst, dst, fs.at[0], recv, b, p1).wait_recv()

    rows = vals.shape[0]
    panel_blocks = GROUP * rows
    dead = SPAN * panel_blocks

    def piece(panel, member):
        return win.at[pl.ds(panel * panel_blocks + member * rows, rows)]

    def tiles(member, c):
        return vbuf.at[pl.ds((member * rows + c) * SLOTS, SLOTS)]

    mine = columns(feats, g)
    for slot, p in enumerate((p2, p3, p1)):
        go(remote(columns(feats, group_of(p)), piece(2, r), fs.at[slot], fr.at[r], b, p))
    go(remote(mine, piece(1, r), us.at[0], ur.at[r], up, r_up))
    go(remote(mine, piece(3, r), ds_.at[0], dr.at[r], down, r_down))
    for slot, p in enumerate((p2, p3, p1)):
        go(remote(table, tbuf.at[r], ts.at[slot], tr.at[r], b, p))
    for c in range(rows):
        go(remote(vals.at[c], tiles(r, c), vs.at[0, c], vr.at[r, c], b, p2))
        go(remote(vals.at[c], tiles(r, c), vs.at[1, c], vr.at[r, c], b, p1))
    own = [
        pltpu.make_async_copy(table, tbuf.at[r], loc.at[0]),
        pltpu.make_async_copy(mine, piece(2, r), loc.at[1]),
        pltpu.make_async_copy(weight, wv, loc.at[2]),
        pltpu.make_async_copy(cot, cv, loc.at[3]),
    ] + [pltpu.make_async_copy(vals.at[c], tiles(r, c), loc.at[4 + c]) for c in range(rows)]
    for copy in own:
        copy.start()
    win[dead] = jnp.zeros((TILE, TILE), BF16)
    runs[TILE] = jnp.zeros((TILE, TILE), F32)

    for slot, p in ((1, p1), (2, p2), (3, p3)):
        landed(piece(2, p), fr.at[p])
        go(remote(piece(2, p), piece(1, p), us.at[slot], ur.at[p], up, r_up))
        go(remote(piece(2, p), piece(3, p), ds_.at[slot], dr.at[p], down, r_down))
    for p in panel_peers:
        landed(tbuf.at[p], tr.at[p])
    own[0].wait()
    dest = (tbuf[0] + tbuf[1]) + (tbuf[2] + tbuf[3])
    smv[0] = dest
    for line, value in enumerate(sorted_entries(dest[0:1, :])):
        smv[line + 1] = jnp.broadcast_to(value, (8, TILE))
    to_scalars = pltpu.make_async_copy(smv, tsm, loc.at[0])
    to_scalars.start()

    from_below = partners(r_down)
    from_above = partners(r_up)
    for slot in range(GROUP):
        i = from_below[slot]
        landed(piece(1, i), ur.at[i])
        go(remote(piece(1, i), piece(0, i), us2.at[slot], ur2.at[i], up, r_up))
        i = from_above[slot]
        landed(piece(3, i), dr.at[i])
        go(remote(piece(3, i), piece(4, i), ds2.at[slot], dr2.at[i], down, r_down))

    def tiles_on(c):
        landed(tiles(p2, c), vr.at[p2, c])
        go(remote(tiles(p2, c), tiles(p2, c), vs.at[2, c], vr.at[p2, c], b, p1))

    half = rows // 2
    for c in range(half):
        tiles_on(c)
    for i in range(GROUP):
        landed(piece(0, i), ur2.at[i])
        landed(piece(4, i), dr2.at[i])
    for copy in own[1:]:
        copy.wait()
    to_scalars.wait()

    halves = [pl.ds(h * half * TILE, half * TILE) for h in range(2)]
    stay = []
    for h in range(2):
        for c in range(h * half, (h + 1) * half):
            if h == 1:
                tiles_on(c)
            landed(tiles(p1, c), vr.at[p1, c])
        for c in range(h * half, (h + 1) * half):
            landed(tiles(p3, c), vr.at[p3, c])
        for slot, q in enumerate(order):

            def one_row(kk, carry, q=q):
                first = (q * rows + kk) * SLOTS
                left = [vbuf[first + s] for s in range(SLOTS)]
                right = [win[tsm[0, 0, first + s]] for s in range(SLOTS)]
                total = jnp.dot(
                    jnp.concatenate(left, axis=1), jnp.concatenate(right, axis=0), preferred_element_type=F32
                )
                aggs[q, pl.ds(pl.multiple_of(kk * TILE, TILE), TILE), :] = total.astype(BF16)
                return carry

            lax.fori_loop(h * half, (h + 1) * half, one_row, 0)
            block, dst = aggs.at[q, halves[h]], aggr.at[g, halves[h]]
            if slot < 3:
                go(remote(block, dst, asend.at[slot, h], arecv.at[g, h], b, q))
            else:
                stay.append(pltpu.make_async_copy(block, dst, loc.at[4 + h]))
                stay[-1].start()

    def dense(t, carry):
        span = pl.ds(pl.multiple_of(t * TILE, TILE), TILE)
        agg = jnp.concatenate([aggr[i, span, :] for i in range(GROUP)], axis=1)
        pre = jnp.dot(agg, wv[...], preferred_element_type=F32)
        sigma = jax.nn.sigmoid(pre)
        out[span, :] = (pre * sigma).astype(BF16)
        slant = cv[span, :].astype(F32) * (sigma * (1.0 + pre * (1.0 - sigma)))
        slope[span, :] = slant.astype(BF16)
        return carry

    for h in range(2):
        stay[h].wait()
        for p in panel_peers:
            gp = group_of(p)
            landed(aggr.at[gp, halves[h]], arecv.at[gp, h])
        lax.fori_loop(h * half, (h + 1) * half, dense, 0)
        for slot, q in enumerate(order):
            part = wv[pl.ds(pl.multiple_of(group_of(q) * TILE, TILE), TILE), :]
            for t in range(h * half, (h + 1) * half):
                turned = lax.dot_general(
                    part, slope[pl.ds(t * TILE, TILE), :], (((1,), (1,)), ((), ())), preferred_element_type=F32
                )
                if slot < 3:
                    bts[slot, t] = turned.astype(BF16)
                else:
                    btp[r * rows + t] = turned.astype(BF16)
            if slot < 3:
                block, dst = bts.at[slot, pl.ds(h * half, half)], btp.at[pl.ds(r * rows + h * half, half)]
                go(remote(block, dst, bsend.at[slot, h], brecv.at[r, h], b, q))

    def weight_rows(i):
        wt[i] = lax.dot_general(aggr[i], slope[...], (((0,), (0,)), ((), ())), preferred_element_type=F32)

    for i in range(2):
        theirs = 2 * (1 - core) + i
        weight_rows(theirs)
        go(remote(wt.at[theirs], a0.at[i], w0s.at[i], w0r.at[i], b, p1))
    quarter = wt.shape[1]
    for i in range(2):
        weight_rows(2 * core + i)
    for i in range(2):
        landed(a0.at[i], w0r.at[i])
        s0[pl.ds(i * quarter, quarter), :] = wt[2 * core + i] + a0[i]
    block = 2 * quarter // deep
    for slot, i in enumerate(tall):
        part = s0.at[pl.ds(pl.multiple_of(i * block, block), block), :]
        go(remote(part, a1.at[y], w1s.at[slot], w1r.at[y], *at_y(i)))
    for p in panel_peers:
        for h in range(2):
            landed(btp.at[pl.ds(p * rows + h * half, half)], brecv.at[p, h])

    def eight(t, carry):
        first = t * 8
        terms = [
            jnp.dot(btp[tsm[3, 0, first + i]], vbuf[tsm[1, 0, first + i]], preferred_element_type=F32)
            for i in range(8)
        ]
        for i in range(8):
            runs[first + i] = terms[i] + runs[tsm[2, 0, first + i]]
        return carry

    lax.fori_loop(0, panel_blocks * SLOTS // 8, eight, 0)

    def share(panel, q, t):
        return runs[tsm[4, 0, panel * panel_blocks + q * rows + t]]

    order_below = ordered(r_down)
    order_above = ordered(r_up)
    steps = 2 * GROUP

    def tiles_of(members, step):
        q, h = members[step // 2], step % 2
        return q, q * 2 + h, range(h * half, (h + 1) * half)

    def outward(step):
        q, i, span = tiles_of(order, step)
        for j, t in enumerate(span):
            far[0, i, j] = share(4, q, t).astype(BF16)
            far[1, i, j] = share(0, q, t).astype(BF16)
        go(remote(far.at[0, i], ru2.at[i], vus.at[step], vur.at[i], up, r_up))
        go(remote(far.at[1, i], rd2.at[i], vds.at[step], vdr.at[i], down, r_down))

    def relay(step):
        q, i, span = tiles_of(order_below, step)
        landed(ru2.at[i], vur.at[i])
        for j, t in enumerate(span):
            su[i, j] = (ru2[i, j].astype(F32) + share(3, q, t)).astype(BF16)
        go(remote(su.at[i], ru1.at[i], vus2.at[step], vur2.at[i], up, r_up))
        q, i, span = tiles_of(order_above, step)
        landed(rd2.at[i], vdr.at[i])
        for j, t in enumerate(span):
            sd[i, j] = (rd2[i, j].astype(F32) + share(1, q, t)).astype(BF16)
        go(remote(sd.at[i], rd1.at[i], vds2.at[step], vdr2.at[i], down, r_down))

    def finish(step):
        q, i, span = tiles_of(order, step)
        h = step % 2
        landed(ru1.at[i], vur2.at[i])
        landed(rd1.at[i], vdr2.at[i])
        for j, t in enumerate(span):
            total = share(2, q, t) + (ru1[i, j].astype(F32) + rd1[i, j].astype(F32))
            if step < steps - 2:
                tot[i, j] = total.astype(BF16)
            else:
                rt[g * 2 + h, j] = total.astype(BF16)
        if step < steps - 2:
            go(remote(tot.at[i], rt.at[g * 2 + h], gs.at[step], gr.at[g * 2 + h], b, q))

    line = block // GROUP
    lanes = min(run, 4)
    high, broad = line // (run // lanes), wt.shape[2] // lanes

    def corner(ref, i):
        return ref.at[
            pl.ds(pl.multiple_of((i // lanes) * high, high), high),
            pl.ds(pl.multiple_of((i % lanes) * broad, broad), broad),
        ]

    def over_x():
        total = s0[pl.ds(pl.multiple_of(y * block, block), block), :]
        for i in tall:
            landed(a1.at[i], w1r.at[i])
            total = total + a1[i]
        s1[...] = total
        for slot, i in enumerate(wide):
            part = s1.at[pl.ds(pl.multiple_of(i * line, line), line), :]
            go(remote(part, a2.at[xi], w2s.at[slot], w2r.at[xi], *at_x(i)))

    def over_z():
        total = s1[pl.ds(pl.multiple_of(xi * line, line), line), :]
        for i in wide:
            landed(a2.at[i], w2r.at[i])
            total = total + a2[i]
        s2[...] = total
        for slot, i in enumerate(along):
            go(remote(corner(s2, i), a3.at[z], w3s.at[slot], w3r.at[z], *at_z(i)))

    def back_z():
        total = corner(s2, z)[...]
        for i in along:
            landed(a3.at[i], w3r.at[i])
            total = total + a3[i]
        corner(b3, z)[...] = total * scale
        for slot, i in enumerate(along):
            go(remote(corner(b3, z), corner(b3, z), x3s.at[slot], x3r.at[z], *at_z(i)))

    def back_x():
        for i in along:
            landed(corner(b3, i), x3r.at[i])
        whole[core, y, xi] = b3[...].astype(BF16)
        mine = whole.at[core, y, xi]
        for slot, i in enumerate(wide):
            go(remote(mine, mine, x2s.at[slot], x2r.at[xi], *at_x(i)))

    def hand_over(i, slot):
        theirs = whole.at[core, i]
        go(remote(theirs, theirs, x0s.at[slot], x0r.at[i], b, p1))

    def back_y():
        for i in wide:
            landed(whole.at[core, y, i], x2r.at[i])
        mine = whole.at[core, y]
        for slot, i in enumerate(tall):
            go(remote(mine, mine, x1s.at[slot], x1r.at[y], *at_y(i)))
        hand_over(y, 0)

    def back_core():
        for slot, i in enumerate(tall):
            landed(whole.at[core, i], x1r.at[i])
            hand_over(i, slot + 1)

    turns = {"o": iter(range(steps)), "r": iter(range(steps)), "f": iter(range(steps))}
    acts = {"o": outward, "r": relay, "f": finish}
    once = {"X": over_x, "Z": over_z, "z": back_z, "x": back_x, "y": back_y, "c": back_core}
    for turn in PLAN:
        if turn in acts:
            acts[turn](next(turns[turn]))
        else:
            once[turn]()

    eye = (
        lax.broadcasted_iota(jnp.int32, (TILE, TILE), 0) == lax.broadcasted_iota(jnp.int32, (TILE, TILE), 1)
    ).astype(BF16)
    for p in panel_peers:
        gp = group_of(p)
        for h in range(2):
            landed(rt.at[gp * 2 + h], gr.at[gp * 2 + h])
    for i in range(GROUP):
        for t in range(rows):
            turned = lax.dot_general(eye, rt[i * 2 + t // half, t % half], (((1,), (1,)), ((), ())), preferred_element_type=F32)
            grad[pl.ds(t * TILE, TILE), pl.ds(i * TILE, TILE)] = turned.astype(BF16)
    for i in range(deep):
        landed(whole.at[1 - core, i], x0r.at[i])
    for c in range(2):
        for i in range(deep):
            for j in range(GROUP):
                wgrad[pl.ds((c * deep + i) * block + j * line, line), :] = whole[c, i, j].astype(F32)
    for copy in sends:
        copy.wait_send()


def window_table(tile_cols, tile_count, panel_blocks, nb):
    center = lax.axis_index("blk")
    offset = (tile_cols // panel_blocks - center) % nb
    offset = jnp.where(offset > REACH, offset - nb, offset)
    index = (offset + REACH) * panel_blocks + tile_cols % panel_blocks
    dead = SPAN * panel_blocks
    alive = jnp.arange(SLOTS, dtype=jnp.int32)[None, :] < tile_count[:, None]
    index = jnp.where(alive, jnp.clip(index, 0, dead - 1), dead).astype(jnp.int32)
    line = jnp.tile(index.reshape(1, -1), (8, GROUP))
    lane = lax.broadcasted_iota(jnp.int32, line.shape, 1)
    return jnp.where(lane // index.size == lax.axis_index("repl"), line, 0)


def local(nb, run, feats, weight, vals, cols, count, cot):
    nodes, width = feats.shape
    rows = nodes // TILE
    panel_blocks = GROUP * rows
    deep = nb // (2 * run)
    table = window_table(cols, count, panel_blocks, nb)
    anywhere = pl.BlockSpec(memory_space=pl.ANY)
    dma = pltpu.SemaphoreType.DMA
    shape = jax.ShapeDtypeStruct
    chunk = (2 * GROUP, rows // 2, TILE, TILE)
    quarter = width // GROUP
    block = 2 * quarter // deep
    line = block // GROUP
    lanes = min(run, 4)
    corner = (line // (run // lanes), width // lanes)
    in_hbm = pl.BlockSpec(memory_space=pltpu.HBM)
    in_vmem = pl.BlockSpec(memory_space=pltpu.VMEM)
    pair = [dma((GROUP,)), dma((GROUP,))]
    out, grad, wgrad = pl.pallas_call(
        functools.partial(layer_kernel, nb, run, 1.0 / math.sqrt(nodes * GROUP * nb)),
        out_shape=(
            shape((nodes, width), BF16),
            shape((nodes, width), BF16),
            shape((width, width), F32),
        ),
        in_specs=[in_hbm, in_hbm, in_hbm, anywhere, in_hbm],
        out_specs=(in_vmem,) * 3,
        scratch_shapes=[
            pltpu.VMEM((SPAN * panel_blocks + 1, TILE, TILE), BF16),
            pltpu.VMEM((panel_blocks * SLOTS, TILE, TILE), BF16),
            pltpu.VMEM((GROUP, 8, TILE), jnp.int32),
            pltpu.VMEM((5, 8, TILE), jnp.int32),
            pltpu.SMEM((5, 8, TILE), jnp.int32),
            pltpu.VMEM((width, width), BF16),
            pltpu.VMEM((nodes, width), BF16),
            pltpu.VMEM((GROUP, nodes, TILE), BF16),
            pltpu.VMEM((GROUP, nodes, TILE), BF16),
            pltpu.VMEM((nodes, width), BF16),
            pltpu.VMEM((GROUP - 1, rows, TILE, TILE), BF16),
            pltpu.VMEM((panel_blocks, TILE, TILE), BF16),
            pltpu.VMEM((GROUP, quarter, width), F32),
            pltpu.VMEM((panel_blocks * SLOTS + 1, TILE, TILE), F32),
            pltpu.VMEM((2,) + chunk, BF16),
        ]
        + [pltpu.VMEM(chunk, BF16)] * 8
        + [
            pltpu.VMEM((2, quarter, width), F32),
            pltpu.VMEM((2 * quarter, width), F32),
            pltpu.VMEM((deep, block, width), F32),
            pltpu.VMEM((block, width), F32),
            pltpu.VMEM((GROUP, line, width), F32),
            pltpu.VMEM((line, width), F32),
            pltpu.VMEM((run,) + corner, F32),
            pltpu.VMEM((line, width), F32),
            pltpu.VMEM((2, deep, GROUP, line, width), BF16),
        ]
        + pair * 5
        + [dma((3, rows)), dma((GROUP, rows))]
        + pair
        + [dma((3, 2)), dma((GROUP, 2))] * 2
        + [dma((2 * GROUP,)), dma((2 * GROUP,))] * 5
        + [dma((2,)), dma((2,))]
        + [dma((deep,)), dma((deep,))]
        + pair
        + [dma((run,)), dma((run,))] * 2
        + pair
        + [dma((deep,)), dma((deep,))] * 2
        + [dma((8,))],
        compiler_params=pltpu.CompilerParams(
            collective_id=0, has_side_effects=True, vmem_limit_bytes=50 << 20
        ),
        name="layer",
    )(
        *(pltpu.with_memory_space_constraint(x, pltpu.HBM) for x in (feats.reshape(rows, TILE, width), weight, vals)),
        table,
        pltpu.with_memory_space_constraint(cot, pltpu.HBM),
    )
    return out, wgrad, grad


def solution(mesh, run=RUN):
    both = ("blk", "repl")
    in_specs = (
        P(both, None),
        P(),
        P(both, None, None, None),
        P(both, None),
        P(both),
        P(both, None),
    )
    out_specs = (P(both, None), P(), P(both, None))
    body = functools.partial(local, mesh.shape["blk"], run)
    return jax.shard_map(body, mesh=mesh, in_specs=in_specs, out_specs=out_specs, check_vma=False)
```
